1024 devices in a mesh: dp: 32 (over y, x), section: 16 (over z), group: 2 (over core).
Axes of the slice: x: 4, y: 8, z: 16, core: 2. Of those that a mesh axis runs over, the one named last changes fastest.
Arguments:
- tokens_in: bfloat16 [8192, 4096], P(('dp', 'group')), may hold values from -6 to 6
- cotangent: bfloat16 [8192, 4096], P(('dp', 'group')), may hold values from -6 to 6
- gains: float32 [16, 4096], P('section'), may hold values from 0.5 to 1.5
- w_qkv: bfloat16 [16, 4096, 384], P('section'), may hold values from -0.09375 to 0.09375
- w_out: bfloat16 [16, 128, 4096], P('section'), may hold values from -0.5 to 0.5
- segments: int32 [512, 16], P(('dp', 'group')), may hold values from 0 to 3, never falling along the last dimension, each value on 1 to 8 neighbouring positions
- plan: int32 [64, 8], P(('dp', 'group')), may hold values from 0 to 7, each once within a row
Outputs:
- input_grads: bfloat16 [16, 8192, 4096], P('section', ('dp', 'group'))
- gain_grads: float32 [16, 4096], P('section')
The draws below stay inside these ranges and needn't reach their ends.
Inputs may be any that keep to these rules, and one draw needn't show every extreme that they name: Each row of plan names every one of 0 .. 7 once. `segments`: segment numbers never fall along a row and every episode lies within one row.
All inputs are finite; a program needn't handle non-finite values.
Results may differ from the reference program's by a relative error of at most 0.029.
Values may be sent and summed in bfloat16 or wider, within the bound.
A program may use at most 32 MiB of HBM per device.

```python
import math
import jax
import jax.numpy as jnp
import numpy as np
from jax import lax

D = 4096
HEAD_DIM = 128
ROW = 16
ROWS_DEV = 8
TOKENS = 8192
N_DP = 32
N_SECTION = 16
N_GROUP = 2


def levels(key, extent, pieces, least, largest):
    loudness, own = 1.0, jax.random.fold_in(key, 6)
    for dim, shards_of in pieces:
        heights = jnp.exp(jax.random.uniform(jax.random.fold_in(own, dim), (shards_of,), jnp.float32, least / len(pieces), largest / len(pieces)))
        loudness = loudness * jnp.repeat(heights, extent[dim] // shards_of).reshape([-1 if axis == dim else 1 for axis in range(len(extent))])
    return loudness


def profile(count, total, most, lean):
    weights = [(1 << 20) // math.isqrt(standing ** lean) + 1 for standing in range(2, count + 1)]
    rest, holding = total - most - (count - 1), [1] * (count - 1)
    while rest > 0:
        movable = [i for i in range(count - 1) if holding[i] < most]
        mass, budget = sum([weights[i] for i in movable]), rest
        for i in movable:
            more = min(most - holding[i], max(1, budget * weights[i] // mass), rest)
            holding[i] = holding[i] + more
            rest = rest - more
    return np.array([most] + holding)


def ragged_sizes(own_key, amount, total, reach, slope):
    if amount == 2:
        one = jax.random.randint(own_key, (), max(1, total - reach), min(reach, total - 1) + 1)
        return jnp.stack([one, total - one])
    lengths = jnp.asarray(profile(amount, total, reach, slope), jnp.int32)
    twos = (amount - 1) // 2
    donor, taker = lengths[1:1 + 2 * twos:2], lengths[2:2 + 2 * twos:2]
    slack = jnp.minimum(donor - 1, reach - taker)
    passed = jax.random.randint(jax.random.fold_in(own_key, 1), (twos,), 0, 1 << 20) % (slack + 1)
    lengths = lengths.at[1:1 + 2 * twos:2].set(donor - passed).at[2:2 + 2 * twos:2].set(taker + passed)
    return lengths[jax.random.permutation(jax.random.fold_in(own_key, 2), amount)]


def centred(stream_key, dims, scale, most, cuts=(), kind=jnp.bfloat16):
    drawn = jax.random.normal(stream_key, dims, jnp.float32) * scale
    if len(cuts) > 0:
        drawn = levels(stream_key, dims, cuts, -0.22, 0.18) * drawn
    return jnp.clip(drawn, min=-most, max=most).astype(kind)


def setup_inputs(seed: int = 0) -> dict:
    seeds = jax.random.split(jax.random.key(seed), 8)
    return {
        "tokens_in": centred(seeds[0], (TOKENS, D), 1.0, 6.0, ((0, 64),)),
        "cotangent": centred(seeds[1], (TOKENS, D), 1.0, 6.0, ((0, 64),)),
        "gains": jnp.clip(0.5 + 1.0 * jax.random.uniform(seeds[2], (N_SECTION, D), jnp.float32) ** levels(seeds[2], (N_SECTION, D), ((0, 16),), -0.2, 0.2), 0.5, 1.5),
        "w_qkv": centred(seeds[3], (N_SECTION, D, 3 * HEAD_DIM), D ** -0.5, 0.09375, ((0, 16),)),
        "w_out": centred(seeds[4], (N_SECTION, HEAD_DIM, D), HEAD_DIM ** -0.5, 0.5, ((0, 16),)),
        "segments": jax.vmap(lambda own: jnp.searchsorted(jnp.cumsum(ragged_sizes(own, 4, ROW, 8, 0)), jnp.arange(ROW), side="right"))(jax.random.split(seeds[5], (TOKENS // ROW))).reshape((TOKENS // ROW, ROW)).astype(jnp.int32),
        "plan": jax.vmap(lambda own: jax.random.permutation(own, ROWS_DEV))(jax.random.split(seeds[6], (N_DP * N_GROUP))).reshape((N_DP * N_GROUP, ROWS_DEV)).astype(jnp.int32),
    }


def attend(hidden, segment, gain_row, w_layer, out_layer):
    count = hidden.shape[0]
    length = hidden.shape[1]
    width = hidden.shape[2]
    head = out_layer.shape[0]
    scaled = hidden * lax.rsqrt(lax.optimization_barrier(jnp.mean(hidden * hidden, axis=-1, keepdims=True)) + 1e-05) * gain_row
    normed = scaled.astype(jnp.bfloat16).reshape(count * length, width)
    projected = jnp.dot(normed, w_layer, preferred_element_type=jnp.float32).reshape(count, length, 3 * head)
    query = projected[:, :, :head]
    keyed = projected[:, :, head:2 * head]
    valued = projected[:, :, 2 * head:]
    positions = jnp.arange(length)
    allowed = (positions[:, None] >= positions[None, :])[None] & (segment[:, :, None] == segment[:, None, :])
    scores = jnp.einsum('rid,rjd->rij', query, keyed, precision=lax.Precision.HIGHEST) / math.sqrt(head)
    scores = jnp.where(allowed, scores, -1e+30)
    weights = jax.nn.softmax(scores, axis=-1)
    mixed = jnp.einsum('rij,rjd->rid', weights, valued, precision=lax.Precision.HIGHEST)
    mixed = mixed.astype(jnp.bfloat16).reshape(count * length, head)
    output = jnp.dot(mixed, out_layer, preferred_element_type=jnp.float32).reshape(count, length, width)
    return hidden + output

def reference(tokens_in, cotangent, gains, w_qkv, w_out, segments, plan):
    width = tokens_in.shape[1]
    share = ROWS_DEV // N_GROUP
    blocks = tokens_in.reshape(N_DP, N_GROUP, ROWS_DEV, ROW, width)
    seg_blocks = segments.reshape(N_DP, N_GROUP, ROWS_DEV, ROW)
    order = plan.reshape(N_DP, N_GROUP, ROWS_DEV)
    chosen = jnp.take_along_axis(blocks, order[:, :, :, None, None], axis=2)
    chosen_seg = jnp.take_along_axis(seg_blocks, order[:, :, :, None], axis=2)
    chosen = chosen.reshape(N_DP, N_GROUP, N_GROUP, share, ROW, width).transpose(0, 2, 1, 3, 4, 5)
    chosen_seg = chosen_seg.reshape(N_DP, N_GROUP, N_GROUP, share, ROW).transpose(0, 2, 1, 3, 4)
    current = chosen.reshape(-1, ROW, width)
    seg_rows = chosen_seg.reshape(-1, ROW)
    inputs = []
    for layer in range(N_SECTION):
        inputs.append(current)
        current = attend(current.astype(jnp.float32), seg_rows, gains[layer], w_qkv[layer], w_out[layer]).astype(jnp.bfloat16)
    incoming = cotangent.reshape(-1, ROW, width)
    grads_x = [None] * N_SECTION
    grads_gain = [None] * N_SECTION
    for layer in reversed(range(N_SECTION)):

        def local_layer(hidden, gain_row):
            return attend(hidden, seg_rows, gain_row, w_qkv[layer], w_out[layer])
        _, pullback = jax.vjp(local_layer, inputs[layer].astype(jnp.float32), gains[layer])
        grad_hidden, grad_gain = pullback(incoming.astype(jnp.float32))
        incoming = grad_hidden.astype(jnp.bfloat16)
        grads_x[layer] = incoming.reshape(-1, width)
        grads_gain[layer] = grad_gain
    return (jnp.stack(grads_x), jnp.stack(grads_gain))
```

```python
import functools
import math

import jax
import jax.numpy as jnp
from jax import lax
from jax.experimental import pallas as pl
from jax.experimental.pallas import tpu as pltpu
from jax.sharding import PartitionSpec as P

MESH = pl.DeviceIdType.MESH
F32 = jnp.float32
BF16 = jnp.bfloat16
CHUNK = 256
BLOCK = 16
AHEAD = 6


def nn(a, b):
    return lax.dot_general(a, b, (((1,), (0,)), ((), ())), preferred_element_type=F32)


def nt(a, b):
    return lax.dot_general(a, b, (((1,), (1,)), ((), ())), preferred_element_type=F32)


def chain_kernel(
    sections, width, spread,
    zt0_ref, et_ref, n0_ref, bias_ref, bg_ref, wqkv_ref, wout_ref, gain_ref, x0_ref, cot_ref,
    out_ref, gsum_ref,
    bgt, zt, a_in, a_own, n_in, n_out, f_in, f_out, s_in, s_out,
    x_in, x_out, c_in,
    mt, m_tok, a_tok, beta_cols,
    q_s, k_s, v_s, p_s, y_s, r_s,
    a_send, a_recv, n_send, n_recv, f_send, f_recv, s_send, s_recv,
    x_send, x_recv, c_send, c_recv,
):
    me = lax.axis_index("section")
    last = sections - 1
    up = lax.rem(me + 1, sections)
    down = lax.rem(me + sections - 1, sections)
    head = a_own.shape[0]
    chunks, tokens, wide = x_in.shape
    rows_in_head = head // BLOCK
    scale = 1.0 / math.sqrt(head)

    barrier = pltpu.get_barrier_semaphore()
    pl.semaphore_signal(barrier, inc=1, device_id={"section": up}, device_id_type=MESH)
    pl.semaphore_signal(barrier, inc=1, device_id={"section": down}, device_id_type=MESH)

    def copy_to(src, dst, ssem, rsem, where):
        return pltpu.make_async_remote_copy(
            src_ref=src, dst_ref=dst, send_sem=ssem, recv_sem=rsem,
            device_id={"section": where}, device_id_type=MESH,
        )

    def a_relay(t):
        return copy_to(a_in.at[t], a_in.at[t], a_send.at[t], a_recv.at[t], up)

    def a_first():
        return copy_to(a_own, a_in.at[me], a_send.at[me], a_recv.at[me], up)

    def n_copy():
        return copy_to(n_out, n_in, n_send, n_recv, up)

    def f_copy(t):
        return copy_to(f_out.at[t], f_in.at[t], f_send.at[t], f_recv.at[t], down)

    def s_copy():
        return copy_to(s_out, s_in, s_send, s_recv, down)

    def x_copy(k):
        return copy_to(x_out.at[k], x_in.at[k], x_send.at[k], x_recv.at[k], up)

    def c_copy(k):
        return copy_to(out_ref.at[k], c_in.at[k], c_send.at[k], c_recv.at[k], down)

    def block_of(t):
        low, high = lax.rem(t, spread), lax.div(t, spread)
        start = pl.multiple_of(low * rows_in_head, rows_in_head)
        return bg_ref[pl.ds(start, rows_in_head), high].reshape(head, 4 * head)

    zt[...] = zt0_ref[...]

    def turn(t, carry):
        bgt[t] = block_of(t).T
        return carry

    lax.fori_loop(0, me, turn, 0)

    @pl.when(me == 0)
    def _():
        n_in[...] = n0_ref[...]
        for k in range(chunks):
            x_in[k] = x0_ref[:, k * wide : (k + 1) * wide]

    @pl.when(me == last)
    def _():
        for k in range(chunks):
            c_in[k] = cot_ref[:, k * wide : (k + 1) * wide]
        s_in[...] = jnp.zeros_like(s_in)
        f_in[last] = jnp.zeros_like(f_in[last])

    pl.semaphore_wait(barrier, 2)

    def gather(t, carry):
        a_relay(t).wait_recv()

        @pl.when(me < last)
        def _():
            a_relay(t).start()

        zt[...] += nn(bgt[t], a_in[t])
        return carry

    lax.fori_loop(0, me, gather, 0)

    @pl.when(me > 0)
    def _():
        n_copy().wait_recv()

    norm = n_in[0:1, :]
    scale_r = lax.rsqrt(jnp.maximum(norm, 0.0) * (1.0 / width) + 1e-05)
    qt = zt[0:head, :] * scale_r
    kt = zt[head : 2 * head, :] * scale_r
    vt = zt[2 * head : 3 * head, :] * scale_r
    yt = zt[3 * head :, :]
    scores = nn(kt.T.astype(BF16), qt.astype(BF16)) * scale + bias_ref[...]
    top = jnp.max(scores, axis=0, keepdims=True)
    weights = jnp.exp(scores - top)
    weights = weights / jnp.sum(weights, axis=0, keepdims=True)
    mixed = nn(vt.astype(BF16), weights.astype(BF16))
    a_own[...] = mixed.astype(BF16)

    @pl.when(me < last)
    def _():
        a_first().start()

    at = a_own[...]
    self_block = block_of(me)[:, 3 * head :]
    y1 = yt + nn(self_block, at)
    moved = norm + jnp.sum(at.astype(F32) * (yt + y1), axis=0, keepdims=True)
    n_out[...] = jnp.broadcast_to(moved, n_out.shape)

    @pl.when(me < last)
    def _():
        n_copy().start()

    q_s[...] = qt
    k_s[...] = kt
    v_s[...] = vt
    p_s[...] = weights
    y_s[...] = y1
    r_s[...] = jnp.broadcast_to(scale_r, r_s.shape)
    a_tok[...] = at.astype(F32).T.astype(BF16)

    def x_step(k, carry):
        @pl.when(me > 0)
        def _():
            x_copy(k).wait_recv()

        @pl.when(me < last)
        def _():
            lane = pl.multiple_of(k * wide, wide)
            grown = x_in[k].astype(F32) + nn(a_tok[...], wout_ref[:, pl.ds(lane, wide)])
            x_out[k] = grown.astype(BF16)
            x_copy(k).start()

        return carry

    pause = jnp.minimum(chunks, AHEAD * (last - me))
    lax.fori_loop(0, pause, x_step, 0)

    @pl.when(me < last)
    def _():
        f_copy(me).wait_recv()
        s_copy().wait_recv()

    summed = s_in[0:1, :]
    dat = et_ref[...] - summed * y_s[...] + f_in[me].astype(F32)
    datb = dat.astype(BF16)
    pt = p_s[...]
    dvt = nt(datb, pt.astype(BF16))
    dpt = nn(v_s[...].T.astype(BF16), datb)
    dst = pt * (dpt - jnp.sum(pt * dpt, axis=0, keepdims=True)) * scale
    dstb = dst.astype(BF16)
    dqt = nn(k_s[...].astype(BF16), dstb)
    dkt = nt(q_s[...].astype(BF16), dstb)
    r = r_s[0:1, :]
    inner = jnp.sum(q_s[...] * dqt + k_s[...] * dkt + v_s[...] * dvt, axis=0, keepdims=True)
    beta = r * r * (1.0 / width) * inner
    mt[0:head, :] = (r * dqt).astype(BF16)
    mt[head : 2 * head, :] = (r * dkt).astype(BF16)
    mt[2 * head : 3 * head, :] = (r * dvt).astype(BF16)
    mt[3 * head :, :] = (-summed * a_own[...].astype(F32)).astype(BF16)
    s_out[...] = jnp.broadcast_to(summed + beta, s_out.shape)

    def f_step(i, carry):
        t = me - 1 - i

        @pl.when(me < last)
        def _():
            f_copy(t).wait_recv()

        @pl.when(me == last)
        def _():
            f_in[t] = jnp.zeros_like(f_in[t])

        f_out[t] = (f_in[t].astype(F32) + nn(block_of(t), mt[...])).astype(BF16)
        f_copy(t).start()

        @pl.when(i == 0)
        def _():
            s_copy().start()

        return carry

    lax.fori_loop(0, me, f_step, 0)

    lax.fori_loop(pause, chunks, x_step, 0)

    m_tok[:, 0:head] = mt[0:head, :].astype(F32).T.astype(BF16)
    m_tok[:, head : 2 * head] = mt[head : 2 * head, :].astype(F32).T.astype(BF16)
    m_tok[:, 2 * head :] = mt[2 * head : 3 * head, :].astype(F32).T.astype(BF16)
    beta_cols[...] = jnp.broadcast_to(beta, (tokens, tokens)).T

    def c_step(k, carry):
        @pl.when(me < last)
        def _():
            c_copy(k).wait_recv()

        start = pl.multiple_of(k * wide, wide)
        turned = nt(m_tok[...], wqkv_ref[pl.ds(start, wide), :])
        x = x_in[k].astype(F32)
        fall = jnp.concatenate([beta_cols[...]] * (wide // tokens), axis=1)
        grad = c_in[k].astype(F32) + gain_ref[k] * turned - fall * x
        gsum_ref[k] = jnp.sum(x * turned, axis=0, keepdims=True)
        out_ref[k] = grad.astype(BF16)

        @pl.when(me > 0)
        def _():
            c_copy(k).start()

        return carry

    lax.fori_loop(0, chunks, c_step, 0)

    @pl.when(me < last)
    def _():
        def done_a(t, carry):
            a_relay(t).wait_send()
            return carry

        lax.fori_loop(0, me + 1, done_a, 0)
        n_copy().wait_send()

        def done_x(k, carry):
            x_copy(k).wait_send()
            return carry

        lax.fori_loop(0, chunks, done_x, 0)

    @pl.when(me > 0)
    def _():
        def done_f(t, carry):
            f_copy(t).wait_send()
            return carry

        lax.fori_loop(0, me, done_f, 0)
        s_copy().wait_send()

        def done_c(k, carry):
            c_copy(k).wait_send()
            return carry

        lax.fori_loop(0, chunks, done_c, 0)


def run_chain(sections, zt0, et, n0, bias, bg, wqkv, wout, gain, x0, cot):
    tokens, width = x0.shape
    head = wout.shape[0]
    chunks = width // CHUNK
    spread = bg.shape[0] * BLOCK // head
    vmem = pl.BlockSpec(memory_space=pltpu.VMEM)
    dma = pltpu.SemaphoreType.DMA
    square = (head, tokens)
    return pl.pallas_call(
        functools.partial(chain_kernel, sections, width, spread),
        out_shape=(
            jax.ShapeDtypeStruct((chunks, tokens, CHUNK), BF16),
            jax.ShapeDtypeStruct((chunks, 1, CHUNK), F32),
        ),
        in_specs=[vmem] * 10,
        out_specs=(vmem, vmem),
        scratch_shapes=[
            pltpu.VMEM((sections, 4 * head, head), BF16),
            pltpu.VMEM((4 * head, tokens), F32),
            pltpu.VMEM((sections, *square), BF16),
            pltpu.VMEM(square, BF16),
            pltpu.VMEM((8, tokens), F32),
            pltpu.VMEM((8, tokens), F32),
            pltpu.VMEM((sections, *square), BF16),
            pltpu.VMEM((sections, *square), BF16),
            pltpu.VMEM((8, tokens), F32),
            pltpu.VMEM((8, tokens), F32),
            pltpu.VMEM((chunks, tokens, CHUNK), BF16),
            pltpu.VMEM((chunks, tokens, CHUNK), BF16),
            pltpu.VMEM((chunks, tokens, CHUNK), BF16),
            pltpu.VMEM((4 * head, tokens), BF16),
            pltpu.VMEM((tokens, 3 * head), BF16),
            pltpu.VMEM((tokens, head), BF16),
            pltpu.VMEM((tokens, tokens), F32),
            pltpu.VMEM(square, F32),
            pltpu.VMEM(square, F32),
            pltpu.VMEM(square, F32),
            pltpu.VMEM((tokens, tokens), F32),
            pltpu.VMEM(square, F32),
            pltpu.VMEM((8, tokens), F32),
            dma((sections,)), dma((sections,)), dma, dma,
            dma((sections,)), dma((sections,)), dma, dma,
            dma((chunks,)), dma((chunks,)), dma((chunks,)), dma((chunks,)),
        ],
        compiler_params=pltpu.CompilerParams(
            collective_id=0, has_side_effects=True, vmem_limit_bytes=48 << 20
        ),
    )(zt0, et, n0, bias, bg, wqkv, wout, gain, x0, cot)


def exchanged(array):
    return lax.all_to_all(array, "group", split_axis=0, concat_axis=0, tiled=True)


def local(tokens_in, cotangent, gains, w_qkv, w_out, segments, plan):
    sections = lax.axis_size("section")
    plane = lax.axis_size(("dp", "group"))
    place = lax.axis_index(("dp", "group"))
    rows_dev = plan.shape[1]
    width = tokens_in.shape[1]
    row_len = segments.shape[1]
    tokens = rows_dev * row_len
    gain, wqkv, wout = gains[0], w_qkv[0], w_out[0]
    head = wout.shape[0]
    chunks = width // CHUNK

    blocks = head // BLOCK
    spread = plane // blocks
    each = sections // spread
    own_rows = lax.dynamic_slice_in_dim(wout, lax.rem(place, blocks) * BLOCK, BLOCK, 0)
    all_rows = lax.all_gather(own_rows, "section").reshape(each, spread, BLOCK, width)
    mine = lax.dynamic_index_in_dim(all_rows, lax.div(place, blocks), 1, keepdims=False)
    scaled = (wqkv.astype(F32) * gain[:, None]).astype(BF16)
    both = jnp.concatenate([scaled, wout.T], axis=1)
    piece = nn(mine.reshape(each * BLOCK, width), both).astype(BF16).reshape(each, BLOCK, 4 * head)
    bg = lax.all_gather(piece, ("dp", "group"))

    rows = jnp.take(tokens_in.reshape(rows_dev, row_len, width), plan[0], axis=0)
    segs = jnp.take(segments, plan[0], axis=0).astype(BF16)
    x0 = exchanged(rows).reshape(tokens, width)
    seg = exchanged(segs).reshape(tokens)

    zt0 = lax.dot_general(both, x0, (((0,), (1,)), ((), ())), preferred_element_type=F32)
    et = nt(wout, cotangent)
    n0 = jnp.broadcast_to(jnp.sum(jnp.square(x0.astype(F32)), axis=1)[None], (8, tokens))
    at = jnp.arange(tokens)
    allowed = (
        (at[:, None] <= at[None, :])
        & (at[:, None] // row_len == at[None, :] // row_len)
        & (seg[:, None] == seg[None, :])
    )
    bias = jnp.where(allowed, 0.0, -1e30).astype(F32)

    grads, gsum = run_chain(
        sections, zt0, et, n0, bias, bg, wqkv, wout, gain.reshape(chunks, 1, CHUNK), x0, cotangent
    )
    grads = grads.transpose(1, 0, 2).reshape(1, tokens, width)
    gain_whole = lax.psum(gsum.reshape(1, width), ("dp", "group"))
    return grads, gain_whole


def solution(mesh):
    placed = (
        P(("dp", "group"), None),
        P(("dp", "group"), None),
        P("section", None),
        P("section", None, None),
        P("section", None, None),
        P(("dp", "group"), None),
        P(("dp", "group"), None),
    )
    return jax.shard_map(
        local,
        mesh=mesh,
        in_specs=placed,
        out_specs=(P("section", ("dp", "group"), None), P("section", None)),
        check_vma=False,
    )
```

```python
import functools
import math

import jax
import jax.numpy as jnp
from jax import lax
from jax.experimental import pallas as pl
from jax.experimental.pallas import tpu as pltpu
from jax.sharding import PartitionSpec as P

MESH = pl.DeviceIdType.MESH
F32 = jnp.float32
BF16 = jnp.bfloat16
CHUNK = 256
BLOCK = 16
PIECES = 4
ALONG_X = 4
AHEAD = 6


def nn(a, b):
    return lax.dot_general(a, b, (((1,), (0,)), ((), ())), preferred_element_type=F32)


def nt(a, b):
    return lax.dot_general(a, b, (((1,), (1,)), ((), ())), preferred_element_type=F32)


def chain_kernel(
    sections, along_y, row_len,
    rows_ref, segs_ref, wqkv_ref, wout_ref, gain_ref, cot_ref,
    out_ref, gtotal_ref,
    x0, seg_in, zb, bg, bgt, zt, et, bias, a_in, a_own, n_in, n_out, f_in, f_out, s_in, s_out,
    x_in, x_out, c_in,
    mt, m_tok, a_tok, beta_cols,
    q_s, k_s, v_s, p_s, y_s, r_s,
    g_own, g_pair, g_x, g_y,
    e_send, e_recv, z_send, z_recv, by_send, by_recv, bx_send, bx_recv, bc_send, bc_recv,
    a_send, a_recv, n_send, n_recv, f_send, f_recv, s_send, s_recv,
    x_send, x_recv, c_send, c_recv,
    gp_send, gp_recv, gx_send, gx_recv, gy_send, gy_recv,
):
    me = lax.axis_index("section")
    place = lax.axis_index("dp")
    core = lax.axis_index("group")
    my_y, my_x = lax.div(place, ALONG_X), lax.rem(place, ALONG_X)
    last = sections - 1
    up = lax.rem(me + 1, sections)
    down = lax.rem(me + sections - 1, sections)
    other = 1 - core
    head = a_own.shape[0]
    chunks, tokens, wide = x_in.shape
    width = chunks * wide
    each = sections // along_y
    mine = core * ALONG_X + my_x
    scale = 1.0 / math.sqrt(head)

    def y_peer(d):
        return lax.rem(my_y + d, along_y) * ALONG_X + my_x

    def x_peer(d):
        return my_y * ALONG_X + lax.rem(my_x + d, ALONG_X)

    barrier = pltpu.get_barrier_semaphore()
    peers = [{"section": up}, {"section": down}, {"group": other}]
    peers += [{"dp": y_peer(d)} for d in range(1, along_y)]
    peers += [{"dp": x_peer(d)} for d in range(1, ALONG_X)]
    for peer in peers:
        pl.semaphore_signal(barrier, inc=1, device_id=peer, device_id_type=MESH)

    def copy_to(src, dst, ssem, rsem, where):
        return pltpu.make_async_remote_copy(
            src_ref=src, dst_ref=dst, send_sem=ssem, recv_sem=rsem,
            device_id=where, device_id_type=MESH,
        )

    def rows_copy():
        return copy_to(
            rows_ref.at[other], x0.at[core], e_send.at[0], e_recv.at[0], {"group": other}
        )

    def segs_copy():
        return copy_to(
            segs_ref.at[other], seg_in.at[core], e_send.at[1], e_recv.at[1], {"group": other}
        )

    def z_copy(h, p):
        return copy_to(
            zb.at[h, p], zb.at[h, p], z_send.at[h, p], z_recv.at[h, p], {"section": up}
        )

    def by_copy(h, d):
        t = my_y + along_y * h
        return copy_to(
            bg.at[t, mine], bg.at[t, mine], by_send.at[h, d], by_recv.at[t], {"dp": y_peer(d)}
        )

    def by_arrival(t):
        return copy_to(
            bg.at[t, mine], bg.at[t, mine], by_send.at[0, 0], by_recv.at[t], {"dp": y_peer(1)}
        )

    def bx_copy(t, d):
        return copy_to(
            bg.at[t, mine], bg.at[t, mine], bx_send.at[t, d], bx_recv.at[t, d], {"dp": x_peer(d)}
        )

    def bc_copy(t):
        half = pl.ds(core * ALONG_X, ALONG_X)
        return copy_to(
            bg.at[t, half], bg.at[t, half], bc_send.at[t], bc_recv.at[t], {"group": other}
        )

    def a_relay(t):
        return copy_to(a_in.at[t], a_in.at[t], a_send.at[t], a_recv.at[t], {"section": up})

    def a_first():
        return copy_to(a_own, a_in.at[me], a_send.at[me], a_recv.at[me], {"section": up})

    def n_copy():
        return copy_to(n_out, n_in, n_send, n_recv, {"section": up})

    def f_copy(t):
        return copy_to(f_out.at[t], f_in.at[t], f_send.at[t], f_recv.at[t], {"section": down})

    def s_copy():
        return copy_to(s_out, s_in, s_send, s_recv, {"section": down})

    def x_copy(k):
        return copy_to(x_out.at[k], x_in.at[k], x_send.at[k], x_recv.at[k], {"section": up})

    def lanes(k):
        return pl.ds(pl.multiple_of(k * wide, wide), wide)

    def c_copy(k):
        return copy_to(
            out_ref.at[:, lanes(k)], c_in.at[k], c_send.at[k], c_recv.at[k], {"section": down}
        )

    def gp_copy():
        return copy_to(g_own, g_pair, gp_send, gp_recv, {"group": other})

    def gx_copy(d):
        return copy_to(
            g_x.at[my_x], g_x.at[my_x], gx_send.at[d], gx_recv.at[d], {"dp": x_peer(d)}
        )

    def gy_copy(d):
        return copy_to(
            g_y.at[my_y], g_y.at[my_y], gy_send.at[d], gy_recv.at[d], {"dp": y_peer(d)}
        )

    def block_of(t):
        return bg[t].reshape(head, 4 * head)

    piece = width // PIECES
    for h in range(each):

        @pl.when(me == my_y + along_y * h)
        def _():
            start = pl.multiple_of(mine * BLOCK, BLOCK)
            for p in range(PIECES):
                zb[h, p] = wout_ref[pl.ds(start, BLOCK), p * piece : (p + 1) * piece]

    pl.semaphore_wait(barrier, len(peers))
    rows_copy().start()
    segs_copy().start()
    for h in range(each):

        @pl.when((me == my_y + along_y * h) & (me < last))
        def _():
            for p in range(PIECES):
                z_copy(h, p).start()

    x0[core] = rows_ref[core]
    seg_in[core] = segs_ref[core]
    et[...] = nt(wout_ref[...], cot_ref[...])

    @pl.when(me == last)
    def _():
        for k in range(chunks):
            c_in[k] = cot_ref[:, k * wide : (k + 1) * wide]
        s_in[...] = jnp.zeros_like(s_in)
        f_in[last] = jnp.zeros_like(f_in[last])

    rows_copy().wait_recv()
    segs_copy().wait_recv()

    segment = seg_in[0][0:8, :].astype(F32) + seg_in[1][0:8, :].astype(F32)
    of_query = jnp.broadcast_to(segment[0:1, :], (tokens, tokens))
    of_key = of_query.T
    key = lax.broadcasted_iota(jnp.int32, (tokens, tokens), 0)
    query = lax.broadcasted_iota(jnp.int32, (tokens, tokens), 1)
    allowed = (key <= query) & (key // row_len == query // row_len) & (of_key == of_query)
    bias[...] = jnp.where(allowed, 0.0, -1e30)

    square = jnp.zeros((tokens, 128), F32)
    grown = jnp.zeros((tokens, 3 * head), F32)
    outer = jnp.zeros((head, tokens), F32)
    for p in range(PIECES):
        cut = slice(p * piece, (p + 1) * piece)
        x = x0[:, :, cut].reshape(tokens, piece)
        wide_x = x.astype(F32)
        grown += nn((wide_x * gain_ref[0:1, cut]).astype(BF16), wqkv_ref[cut, :])
        outer += nt(wout_ref[:, cut], x)
        for i in range(piece // 128):
            part = wide_x[:, i * 128 : (i + 1) * 128]
            square += part * part
    zt[0 : 3 * head, :] = grown.T
    zt[3 * head :, :] = outer

    @pl.when(me == 0)
    def _():
        n_in[...] = jnp.sum(square.T, axis=0, keepdims=True) + jnp.zeros_like(n_in)
        for k in range(chunks):
            x_in[k] = x0[:, :, k * wide : (k + 1) * wide].reshape(tokens, wide)

    for h in reversed(range(each)):
        source = my_y + along_y * h

        @pl.when(me > source)
        def _():
            for p in range(PIECES):
                z_copy(h, p).wait_recv()

                @pl.when(me < last)
                def _():
                    z_copy(h, p).start()

        @pl.when(me >= source)
        def _():
            left = jnp.zeros((BLOCK, 3 * head), F32)
            right = jnp.zeros((BLOCK, head), F32)
            for p in range(PIECES):
                cut = slice(p * piece, (p + 1) * piece)
                rows = zb[h, p]
                left += nn((rows.astype(F32) * gain_ref[0:1, cut]).astype(BF16), wqkv_ref[cut, :])
                right += nt(rows, wout_ref[:, cut])
            bg[source, mine] = jnp.concatenate([left, right], axis=1).astype(BF16)
            for d in range(1, along_y):
                by_copy(h, d).start()

    def over_x(t, carry):
        @pl.when(lax.rem(t, along_y) != my_y)
        def _():
            by_arrival(t).wait_recv()

        for d in range(1, ALONG_X):
            bx_copy(t, d).start()
        return carry

    lax.fori_loop(0, me + 1, over_x, 0)

    def over_cores(t, carry):
        for d in range(1, ALONG_X):
            bx_copy(t, d).wait_recv()
        bc_copy(t).start()
        return carry

    lax.fori_loop(0, me + 1, over_cores, 0)

    def turn(t, carry):
        bc_copy(t).wait_recv()
        bgt[t] = block_of(t).T
        return carry

    lax.fori_loop(0, me + 1, turn, 0)

    def gather(t, carry):
        a_relay(t).wait_recv()

        @pl.when(me < last)
        def _():
            a_relay(t).start()

        zt[...] += nn(bgt[t], a_in[t])
        return carry

    lax.fori_loop(0, me, gather, 0)

    @pl.when(me > 0)
    def _():
        n_copy().wait_recv()

    norm = n_in[0:1, :]
    scale_r = lax.rsqrt(jnp.maximum(norm, 0.0) * (1.0 / width) + 1e-05)
    qt = zt[0:head, :] * scale_r
    kt = zt[head : 2 * head, :] * scale_r
    vt = zt[2 * head : 3 * head, :] * scale_r
    yt = zt[3 * head :, :]
    scores = nn(kt.T.astype(BF16), qt.astype(BF16)) * scale + bias[...]
    top = jnp.max(scores, axis=0, keepdims=True)
    weights = jnp.exp(scores - top)
    weights = weights / jnp.sum(weights, axis=0, keepdims=True)
    mixed = nn(vt.astype(BF16), weights.astype(BF16))
    a_own[...] = mixed.astype(BF16)

    @pl.when(me < last)
    def _():
        a_first().start()

    at = a_own[...]
    self_block = block_of(me)[:, 3 * head :]
    y1 = yt + nn(self_block, at)
    moved = norm + jnp.sum(at.astype(F32) * (yt + y1), axis=0, keepdims=True)
    n_out[...] = jnp.broadcast_to(moved, n_out.shape)

    @pl.when(me < last)
    def _():
        n_copy().start()

    q_s[...] = qt
    k_s[...] = kt
    v_s[...] = vt
    p_s[...] = weights
    y_s[...] = y1
    r_s[...] = jnp.broadcast_to(scale_r, r_s.shape)
    a_tok[...] = at.astype(F32).T.astype(BF16)

    def x_step(k, carry):
        @pl.when(me > 0)
        def _():
            x_copy(k).wait_recv()

        @pl.when(me < last)
        def _():
            longer = x_in[k].astype(F32) + nn(a_tok[...], wout_ref[:, lanes(k)])
            x_out[k] = longer.astype(BF16)
            x_copy(k).start()

        return carry

    pause = jnp.minimum(chunks, AHEAD * (last - me))
    lax.fori_loop(0, pause, x_step, 0)

    @pl.when(me < last)
    def _():
        f_copy(me).wait_recv()
        s_copy().wait_recv()

    summed = s_in[0:1, :]
    dat = et[...] - summed * y_s[...] + f_in[me].astype(F32)
    datb = dat.astype(BF16)
    pt = p_s[...]
    dvt = nt(datb, pt.astype(BF16))
    dpt = nn(v_s[...].T.astype(BF16), datb)
    dst = pt * (dpt - jnp.sum(pt * dpt, axis=0, keepdims=True)) * scale
    dstb = dst.astype(BF16)
    dqt = nn(k_s[...].astype(BF16), dstb)
    dkt = nt(q_s[...].astype(BF16), dstb)
    r = r_s[0:1, :]
    inner = jnp.sum(q_s[...] * dqt + k_s[...] * dkt + v_s[...] * dvt, axis=0, keepdims=True)
    beta = r * r * (1.0 / width) * inner
    mt[0:head, :] = (r * dqt).astype(BF16)
    mt[head : 2 * head, :] = (r * dkt).astype(BF16)
    mt[2 * head : 3 * head, :] = (r * dvt).astype(BF16)
    mt[3 * head :, :] = (-summed * a_own[...].astype(F32)).astype(BF16)
    s_out[...] = jnp.broadcast_to(summed + beta, s_out.shape)

    def f_step(i, carry):
        t = me - 1 - i

        @pl.when(me < last)
        def _():
            f_copy(t).wait_recv()

        @pl.when(me == last)
        def _():
            f_in[t] = jnp.zeros_like(f_in[t])

        f_out[t] = (f_in[t].astype(F32) + nn(block_of(t), mt[...])).astype(BF16)
        f_copy(t).start()

        @pl.when(i == 0)
        def _():
            s_copy().start()

        return carry

    lax.fori_loop(0, me, f_step, 0)

    lax.fori_loop(pause, chunks, x_step, 0)

    m_tok[:, 0:head] = mt[0:head, :].astype(F32).T.astype(BF16)
    m_tok[:, head : 2 * head] = mt[head : 2 * head, :].astype(F32).T.astype(BF16)
    m_tok[:, 2 * head :] = mt[2 * head : 3 * head, :].astype(F32).T.astype(BF16)
    beta_cols[...] = jnp.broadcast_to(beta, (tokens, tokens)).T

    def c_step(k, carry):
        @pl.when(me < last)
        def _():
            c_copy(k).wait_recv()

        start = pl.multiple_of(k * wide, wide)
        turned = nt(m_tok[...], wqkv_ref[pl.ds(start, wide), :])
        x = x_in[k].astype(F32)
        fall = jnp.concatenate([beta_cols[...]] * (wide // tokens), axis=1)
        grad = c_in[k].astype(F32) + gain_ref[0:1, lanes(k)] * turned - fall * x
        g_own[pl.ds(k, 1), :] = jnp.sum(x * turned, axis=0, keepdims=True)
        out_ref[:, lanes(k)] = grad.astype(BF16)

        @pl.when(me > 0)
        def _():
            c_copy(k).start()

        return carry

    lax.fori_loop(0, chunks, c_step, 0)

    gp_copy().start()
    gp_copy().wait_recv()
    g_x[my_x] = g_own[...] + g_pair[...]
    for d in range(1, ALONG_X):
        gx_copy(d).start()
    for d in range(1, ALONG_X):
        gx_copy(d).wait_recv()
    total = g_x[0]
    for i in range(1, ALONG_X):
        total += g_x[i]
    g_y[my_y] = total
    for d in range(1, along_y):
        gy_copy(d).start()
    for d in range(1, along_y):
        gy_copy(d).wait_recv()
    total = g_y[0]
    for i in range(1, along_y):
        total += g_y[i]
    gtotal_ref[...] = total

    rows_copy().wait_send()
    segs_copy().wait_send()
    gp_copy().wait_send()
    for d in range(1, ALONG_X):
        gx_copy(d).wait_send()
    for d in range(1, along_y):
        gy_copy(d).wait_send()
    for h in range(each):

        @pl.when(me >= my_y + along_y * h)
        def _():
            for d in range(1, along_y):
                by_copy(h, d).wait_send()

            @pl.when(me < last)
            def _():
                for p in range(PIECES):
                    z_copy(h, p).wait_send()

    def done_b(t, carry):
        for d in range(1, ALONG_X):
            bx_copy(t, d).wait_send()
        bc_copy(t).wait_send()
        return carry

    lax.fori_loop(0, me + 1, done_b, 0)

    @pl.when(me < last)
    def _():
        def done_a(t, carry):
            a_relay(t).wait_send()
            return carry

        lax.fori_loop(0, me + 1, done_a, 0)
        n_copy().wait_send()

        def done_x(k, carry):
            x_copy(k).wait_send()
            return carry

        lax.fori_loop(0, chunks, done_x, 0)

    @pl.when(me > 0)
    def _():
        def done_f(t, carry):
            f_copy(t).wait_send()
            return carry

        lax.fori_loop(0, me, done_f, 0)
        s_copy().wait_send()

        def done_c(k, carry):
            c_copy(k).wait_send()
            return carry

        lax.fori_loop(0, chunks, done_c, 0)


def run_chain(sections, along_y, row_len, rows, segs, wqkv, wout, gain, cot):
    tokens, width = cot.shape
    head = wout.shape[0]
    chunks = width // CHUNK
    each = sections // along_y
    blocks = head // BLOCK
    vmem = pl.BlockSpec(memory_space=pltpu.VMEM)
    dma = pltpu.SemaphoreType.DMA
    square = (head, tokens)
    return pl.pallas_call(
        functools.partial(chain_kernel, sections, along_y, row_len),
        out_shape=(
            jax.ShapeDtypeStruct((tokens, width), BF16),
            jax.ShapeDtypeStruct((chunks, CHUNK), F32),
        ),
        in_specs=[vmem] * 6,
        out_specs=(vmem, vmem),
        scratch_shapes=[
            pltpu.VMEM(rows.shape, BF16),
            pltpu.VMEM(segs.shape, BF16),
            pltpu.VMEM((each, PIECES, BLOCK, width // PIECES), BF16),
            pltpu.VMEM((sections, blocks, BLOCK, 4 * head), BF16),
            pltpu.VMEM((sections, 4 * head, head), BF16),
            pltpu.VMEM((4 * head, tokens), F32),
            pltpu.VMEM(square, F32),
            pltpu.VMEM((tokens, tokens), F32),
            pltpu.VMEM((sections, *square), BF16),
            pltpu.VMEM(square, BF16),
            pltpu.VMEM((8, tokens), F32),
            pltpu.VMEM((8, tokens), F32),
            pltpu.VMEM((sections, *square), BF16),
            pltpu.VMEM((sections, *square), BF16),
            pltpu.VMEM((8, tokens), F32),
            pltpu.VMEM((8, tokens), F32),
            pltpu.VMEM((chunks, tokens, CHUNK), BF16),
            pltpu.VMEM((chunks, tokens, CHUNK), BF16),
            pltpu.VMEM((chunks, tokens, CHUNK), BF16),
            pltpu.VMEM((4 * head, tokens), BF16),
            pltpu.VMEM((tokens, 3 * head), BF16),
            pltpu.VMEM((tokens, head), BF16),
            pltpu.VMEM((tokens, tokens), F32),
            pltpu.VMEM(square, F32),
            pltpu.VMEM(square, F32),
            pltpu.VMEM(square, F32),
            pltpu.VMEM((tokens, tokens), F32),
            pltpu.VMEM(square, F32),
            pltpu.VMEM((8, tokens), F32),
            pltpu.VMEM((chunks, CHUNK), F32),
            pltpu.VMEM((chunks, CHUNK), F32),
            pltpu.VMEM((ALONG_X, chunks, CHUNK), F32),
            pltpu.VMEM((along_y, chunks, CHUNK), F32),
            dma((2,)), dma((2,)), dma((each, PIECES)), dma((each, PIECES)),
            dma((each, along_y)), dma((sections,)),
            dma((sections, ALONG_X)), dma((sections, ALONG_X)),
            dma((sections,)), dma((sections,)),
            dma((sections,)), dma((sections,)), dma, dma,
            dma((sections,)), dma((sections,)), dma, dma,
            dma((chunks,)), dma((chunks,)), dma((chunks,)), dma((chunks,)),
            dma, dma, dma((ALONG_X,)), dma((ALONG_X,)), dma((along_y,)), dma((along_y,)),
        ],
        compiler_params=pltpu.CompilerParams(
            collective_id=0, has_side_effects=True, vmem_limit_bytes=48 << 20
        ),
    )(rows, segs, wqkv, wout, gain, cot)


def local(tokens_in, cotangent, gains, w_qkv, w_out, segments, plan):
    sections = lax.axis_size("section")
    along_y = lax.axis_size("dp") // ALONG_X
    core = lax.axis_index("group")
    rows_dev = plan.shape[1]
    width = tokens_in.shape[1]
    row_len = segments.shape[1]
    half = rows_dev // 2 * row_len

    order = plan[0]
    blocks = tokens_in.reshape(rows_dev, row_len, width)
    rows = blocks.at[order].get(mode="promise_in_bounds").reshape(2, half, width)
    segs = segments.at[order].get(mode="promise_in_bounds").astype(BF16).reshape(2, half)
    spot = jnp.arange(2 * half) // half == core
    segs = jnp.where(spot[None], jnp.concatenate([segs, segs], axis=1), 0)
    segs = jnp.broadcast_to(segs[:, None, :], (2, 16, 2 * half))

    grads, gain_whole = run_chain(
        sections, along_y, row_len, rows, segs, w_qkv[0], w_out[0], gains, cotangent
    )
    return grads[None], gain_whole.reshape(1, width)


def solution(mesh):
    placed = (
        P(("dp", "group"), None),
        P(("dp", "group"), None),
        P("section", None),
        P("section", None, None),
        P("section", None, None),
        P(("dp", "group"), None),
        P(("dp", "group"), None),
    )
    return jax.shard_map(
        local,
        mesh=mesh,
        in_specs=placed,
        out_specs=(P("section", ("dp", "group"), None), P("section", None)),
        check_vma=False,
    )
```

```python
import functools
import math

import jax
import jax.numpy as jnp
from jax import lax
from jax.experimental import pallas as pl
from jax.experimental.pallas import tpu as pltpu
from jax.sharding import PartitionSpec as P

MESH = pl.DeviceIdType.MESH
F32 = jnp.float32
BF16 = jnp.bfloat16
CHUNK = 128
BLOCK = 16
PIECES = 4
ALONG_X = 4
AHEAD = 8
LAG = 3


def nn(a, b):
    return lax.dot_general(a, b, (((1,), (0,)), ((), ())), preferred_element_type=F32)


def nt(a, b):
    return lax.dot_general(a, b, (((1,), (1,)), ((), ())), preferred_element_type=F32)


def chain_kernel(
    sections, along_y, row_len,
    rows_ref, segs_ref, wqkv_ref, wout_ref, gain_ref, cot_ref,
    out_ref, gtotal_ref,
    x0, seg_in, zb, bg, bgt, zt, et, bias, a_in, a_own, n_in, n_out, f_in, f_out, s_in, s_out,
    x_in, x_out, c_in, c_out,
    mt, m_tok, a_tok, sum_cols,
    q_s, k_s, v_s, p_s, y_s, r_s,
    g_own, g_pair, g_x, g_y,
    e_send, e_recv, z_send, z_recv, by_send, by_recv, bx_send, bx_recv, bc_send, bc_recv,
    a_send, a_recv, n_send, n_recv, f_send, f_recv, s_send, s_recv,
    x_send, x_recv, c_send, c_recv,
    gp_send, gp_recv, gx_send, gx_recv, gy_send, gy_recv,
):
    me = lax.axis_index("section")
    place = lax.axis_index("dp")
    core = lax.axis_index("group")
    my_y, my_x = lax.div(place, ALONG_X), lax.rem(place, ALONG_X)
    last = sections - 1
    up = lax.rem(me + 1, sections)
    down = lax.rem(me + sections - 1, sections)
    other = 1 - core
    head = a_own.shape[0]
    chunks, tokens, wide = x_in.shape
    width = chunks * wide
    each = sections // along_y
    mine = core * ALONG_X + my_x
    scale = 1.0 / math.sqrt(head)

    def y_peer(d):
        return lax.rem(my_y + d, along_y) * ALONG_X + my_x

    def x_peer(d):
        return my_y * ALONG_X + lax.rem(my_x + d, ALONG_X)

    barrier = pltpu.get_barrier_semaphore()
    peers = [{"group": other}]
    peers += [{"dp": y_peer(d)} for d in range(1, along_y)]
    peers += [{"dp": x_peer(d)} for d in range(1, ALONG_X)]
    for peer in peers:
        pl.semaphore_signal(barrier, inc=1, device_id=peer, device_id_type=MESH)

    @pl.when(me < last)
    def _():
        pl.semaphore_signal(barrier, inc=1, device_id={"section": up}, device_id_type=MESH)

    @pl.when(me > 0)
    def _():
        pl.semaphore_signal(barrier, inc=1, device_id={"section": down}, device_id_type=MESH)

    def copy_to(src, dst, ssem, rsem, where):
        return pltpu.make_async_remote_copy(
            src_ref=src, dst_ref=dst, send_sem=ssem, recv_sem=rsem,
            device_id=where, device_id_type=MESH,
        )

    def rows_copy():
        return copy_to(
            rows_ref.at[other], x0.at[core], e_send.at[0], e_recv.at[0], {"group": other}
        )

    def segs_copy():
        return copy_to(
            segs_ref.at[other], seg_in.at[core], e_send.at[1], e_recv.at[1], {"group": other}
        )

    def z_copy(h, p):
        return copy_to(
            zb.at[h, p], zb.at[h, p], z_send.at[h, p], z_recv.at[h, p], {"section": up}
        )

    def by_copy(h, d):
        t = my_y + along_y * h
        return copy_to(
            bg.at[t, mine], bg.at[t, mine], by_send.at[h, d], by_recv.at[t], {"dp": y_peer(d)}
        )

    def by_arrival(t):
        return copy_to(
            bg.at[t, mine], bg.at[t, mine], by_send.at[0, 0], by_recv.at[t], {"dp": y_peer(1)}
        )

    def bx_copy(t, d):
        return copy_to(
            bg.at[t, mine], bg.at[t, mine], bx_send.at[t, d], bx_recv.at[t, d], {"dp": x_peer(d)}
        )

    def bc_copy(t):
        half = pl.ds(core * ALONG_X, ALONG_X)
        return copy_to(
            bg.at[t, half], bg.at[t, half], bc_send.at[t], bc_recv.at[t], {"group": other}
        )

    def a_relay(t):
        return copy_to(a_in.at[t], a_in.at[t], a_send.at[t], a_recv.at[t], {"section": up})

    def a_first():
        return copy_to(a_own, a_in.at[me], a_send.at[me], a_recv.at[me], {"section": up})

    def n_copy():
        return copy_to(n_out, n_in, n_send, n_recv, {"section": up})

    def f_copy(t):
        return copy_to(f_out.at[t], f_in.at[t], f_send.at[t], f_recv.at[t], {"section": down})

    def s_copy():
        return copy_to(s_out, s_in, s_send, s_recv, {"section": down})

    def x_copy(k):
        return copy_to(x_out.at[k], x_in.at[k], x_send.at[k], x_recv.at[k], {"section": up})

    def lanes(k):
        return pl.ds(pl.multiple_of(k * wide, wide), wide)

    def c_copy(k):
        return copy_to(
            c_out.at[k], c_in.at[k], c_send.at[k], c_recv.at[k], {"section": down}
        )

    def gp_copy():
        return copy_to(g_own, g_pair, gp_send, gp_recv, {"group": other})

    def gx_copy(d):
        return copy_to(
            g_x.at[my_x], g_x.at[my_x], gx_send.at[d], gx_recv.at[d], {"dp": x_peer(d)}
        )

    def gy_copy(d):
        return copy_to(
            g_y.at[my_y], g_y.at[my_y], gy_send.at[d], gy_recv.at[d], {"dp": y_peer(d)}
        )

    def block_of(t):
        return bg[t].reshape(head, 4 * head)

    piece = width // PIECES
    for h in range(each):

        @pl.when(me == my_y + along_y * h)
        def _():
            start = pl.multiple_of(mine * BLOCK, BLOCK)
            for p in range(PIECES):
                zb[h, p] = wout_ref[pl.ds(start, BLOCK), p * piece : (p + 1) * piece]

    along_z = jnp.where(me < last, 1, 0) + jnp.where(me > 0, 1, 0)
    pl.semaphore_wait(barrier, len(peers) + along_z)
    rows_copy().start()
    segs_copy().start()
    for h in range(each):

        @pl.when((me == my_y + along_y * h) & (me < last))
        def _():
            for p in range(PIECES):
                z_copy(h, p).start()

    x0[core] = rows_ref[core]
    seg_in[core] = segs_ref[core]
    et[...] = nt(wout_ref[...], cot_ref[...])

    @pl.when(me == last)
    def _():
        for k in range(chunks):
            c_in[k] = cot_ref[:, k * wide : (k + 1) * wide]
        s_in[...] = jnp.zeros_like(s_in)
        f_in[last] = jnp.zeros_like(f_in[last])

    rows_copy().wait_recv()
    segs_copy().wait_recv()

    segment = seg_in[0][0:8, :].astype(F32) + seg_in[1][0:8, :].astype(F32)
    of_query = jnp.broadcast_to(segment[0:1, :], (tokens, tokens))
    of_key = of_query.T
    key = lax.broadcasted_iota(jnp.int32, (tokens, tokens), 0)
    query = lax.broadcasted_iota(jnp.int32, (tokens, tokens), 1)
    allowed = (key <= query) & (key // row_len == query // row_len) & (of_key == of_query)
    bias[...] = jnp.where(allowed, 0.0, -1e30)

    square = jnp.zeros((tokens, 128), F32)
    grown = jnp.zeros((tokens, 3 * head), F32)
    outer = jnp.zeros((head, tokens), F32)
    for p in range(PIECES):
        cut = slice(p * piece, (p + 1) * piece)
        x = x0[:, :, cut].reshape(tokens, piece)
        wide_x = x.astype(F32)
        grown += nn((wide_x * gain_ref[0:1, cut]).astype(BF16), wqkv_ref[cut, :])
        outer += nt(wout_ref[:, cut], x)
        for i in range(piece // 128):
            part = wide_x[:, i * 128 : (i + 1) * 128]
            square += part * part
    zt[0 : 3 * head, :] = grown.T
    zt[3 * head :, :] = outer

    @pl.when(me == 0)
    def _():
        n_in[...] = jnp.sum(square.T, axis=0, keepdims=True) + jnp.zeros_like(n_in)
        for k in range(chunks):
            x_in[k] = x0[:, :, k * wide : (k + 1) * wide].reshape(tokens, wide)

    for h in reversed(range(each)):
        source = my_y + along_y * h

        @pl.when(me > source)
        def _():
            for p in range(PIECES):
                z_copy(h, p).wait_recv()

                @pl.when(me < last)
                def _():
                    z_copy(h, p).start()

        @pl.when(me >= source)
        def _():
            left = jnp.zeros((BLOCK, 3 * head), F32)
            right = jnp.zeros((BLOCK, head), F32)
            for p in range(PIECES):
                cut = slice(p * piece, (p + 1) * piece)
                rows = zb[h, p]
                left += nn((rows.astype(F32) * gain_ref[0:1, cut]).astype(BF16), wqkv_ref[cut, :])
                right += nt(rows, wout_ref[:, cut])
            bg[source, mine] = jnp.concatenate([left, right], axis=1).astype(BF16)
            for d in range(1, along_y):
                by_copy(h, d).start()

        top = jnp.minimum(me, along_y * h + along_y - 1)
        count = jnp.maximum(top - along_y * h + 1, 0)

        def flow(i, carry):
            @pl.when(i < count)
            def _():
                t = top - i

                @pl.when(lax.rem(t, along_y) != my_y)
                def _():
                    by_arrival(t).wait_recv()

                for d in range(1, ALONG_X):
                    bx_copy(t, d).start()

            @pl.when((i >= LAG) & (i < count + LAG))
            def _():
                t = top - (i - LAG)
                for d in range(1, ALONG_X):
                    bx_copy(t, d).wait_recv()
                bc_copy(t).start()

            @pl.when(i >= 2 * LAG)
            def _():
                t = top - (i - 2 * LAG)
                bc_copy(t).wait_recv()
                bgt[t] = block_of(t).T

            return carry

        lax.fori_loop(0, jnp.where(count > 0, count + 2 * LAG, 0), flow, 0)

    def gather(t, carry):
        a_relay(t).wait_recv()

        @pl.when(me < last)
        def _():
            a_relay(t).start()

        zt[...] += nn(bgt[t], a_in[t])
        return carry

    lax.fori_loop(0, me, gather, 0)

    @pl.when(me > 0)
    def _():
        n_copy().wait_recv()

    norm = n_in[0:1, :]
    scale_r = lax.rsqrt(jnp.maximum(norm, 0.0) * (1.0 / width) + 1e-05)
    qt = zt[0:head, :] * scale_r
    kt = zt[head : 2 * head, :] * scale_r
    vt = zt[2 * head : 3 * head, :] * scale_r
    yt = zt[3 * head :, :]
    scores = nn(kt.T.astype(BF16), qt.astype(BF16)) * scale + bias[...]
    top = jnp.max(scores, axis=0, keepdims=True)
    weights = jnp.exp(scores - top)
    weights = weights / jnp.sum(weights, axis=0, keepdims=True)
    mixed = nn(vt.astype(BF16), weights.astype(BF16))
    a_own[...] = mixed.astype(BF16)

    @pl.when(me < last)
    def _():
        a_first().start()

    at = a_own[...]
    self_block = block_of(me)[:, 3 * head :]
    y1 = yt + nn(self_block, at)
    moved = norm + jnp.sum(at.astype(F32) * (yt + y1), axis=0, keepdims=True)
    n_out[...] = jnp.broadcast_to(moved, n_out.shape)

    @pl.when(me < last)
    def _():
        n_copy().start()

    q_s[...] = qt
    k_s[...] = kt
    v_s[...] = vt
    p_s[...] = weights
    y_s[...] = y1
    r_s[...] = jnp.broadcast_to(scale_r, r_s.shape)
    a_tok[...] = at.astype(F32).T.astype(BF16)

    def x_step(k, carry):
        @pl.when(me > 0)
        def _():
            x_copy(k).wait_recv()

        @pl.when(me < last)
        def _():
            longer = x_in[k].astype(F32) + nn(a_tok[...], wout_ref[:, lanes(k)])
            x_out[k] = longer.astype(BF16)
            x_copy(k).start()

        return carry

    pause = jnp.minimum(chunks, AHEAD * (last - me))
    lax.fori_loop(0, pause, x_step, 0)

    @pl.when(me < last)
    def _():
        f_copy(me).wait_recv()
        s_copy().wait_recv()

    summed = s_in[0:1, :]
    dat = et[...] - summed * y_s[...] + f_in[me].astype(F32)
    datb = dat.astype(BF16)
    pt = p_s[...]
    dvt = nt(datb, pt.astype(BF16))
    dpt = nn(v_s[...].T.astype(BF16), datb)
    dst = pt * (dpt - jnp.sum(pt * dpt, axis=0, keepdims=True)) * scale
    dstb = dst.astype(BF16)
    dqt = nn(k_s[...].astype(BF16), dstb)
    dkt = nt(q_s[...].astype(BF16), dstb)
    r = r_s[0:1, :]
    inner = jnp.sum(q_s[...] * dqt + k_s[...] * dkt + v_s[...] * dvt, axis=0, keepdims=True)
    beta = r * r * (1.0 / width) * inner
    mt[0:head, :] = (r * dqt).astype(BF16)
    mt[head : 2 * head, :] = (r * dkt).astype(BF16)
    mt[2 * head : 3 * head, :] = (r * dvt).astype(BF16)
    mt[3 * head :, :] = (-summed * a_own[...].astype(F32)).astype(BF16)
    s_out[...] = jnp.broadcast_to(summed + beta, s_out.shape)

    def f_step(i, carry):
        t = me - 1 - i

        @pl.when(me < last)
        def _():
            f_copy(t).wait_recv()

        @pl.when(me == last)
        def _():
            f_in[t] = jnp.zeros_like(f_in[t])

        f_out[t] = (f_in[t].astype(F32) + nn(block_of(t), mt[...])).astype(BF16)
        f_copy(t).start()

        @pl.when(i == 0)
        def _():
            s_copy().start()

        return carry

    lax.fori_loop(0, me, f_step, 0)

    for i in range(4):
        part = slice(i * head, (i + 1) * head)
        m_tok[:, part] = mt[part, :].astype(F32).T.astype(BF16)
    sum_cols[...] = jnp.broadcast_to(summed + beta, (tokens, tokens)).T

    def turned(k):
        start = pl.multiple_of(k * wide, wide)
        return nt(m_tok[:, 0 : 3 * head], wqkv_ref[pl.ds(start, wide), :])

    def gain_step(k, carry):
        g_own[pl.ds(k, 1), :] = jnp.sum(x_in[k].astype(F32) * turned(k), axis=0, keepdims=True)
        return carry

    def gains_0():
        lax.fori_loop(0, chunks, gain_step, 0)
        gp_copy().start()

    def gains_1():
        gp_copy().wait_recv()
        g_x[my_x] = g_own[...] + g_pair[...]
        for d in range(1, ALONG_X):
            gx_copy(d).start()

    def gains_2():
        for d in range(1, ALONG_X):
            gx_copy(d).wait_recv()
        total = g_x[0]
        for i in range(1, ALONG_X):
            total += g_x[i]
        g_y[my_y] = total
        for d in range(1, along_y):
            gy_copy(d).start()

    def gains_3():
        for d in range(1, along_y):
            gy_copy(d).wait_recv()
        total = g_y[0]
        for i in range(1, along_y):
            total += g_y[i]
        gtotal_ref[...] = total

    def c_step(k, carry):
        @pl.when(me < last)
        def _():
            c_copy(k).wait_recv()

        fresh = c_in[k].astype(F32) + gain_ref[0:1, lanes(k)] * turned(k)
        fresh += nn(m_tok[:, 3 * head :], wout_ref[:, lanes(k)])

        @pl.when(me > 0)
        def _():
            c_out[k] = fresh.astype(BF16)
            c_copy(k).start()

        @pl.when(me == 0)
        def _():
            out_ref[:, lanes(k)] = (fresh - sum_cols[...] * x_in[k].astype(F32)).astype(BF16)

        return carry

    def rest_step(k, carry):
        rest = c_out[k].astype(F32) - sum_cols[...] * x_in[k].astype(F32)
        out_ref[:, lanes(k)] = rest.astype(BF16)
        return carry

    stages = (gains_0, gains_1, gains_2, gains_3)
    for i, stage in enumerate(stages):
        pl.when(me == 0)(stage)
        if i < 3:
            lax.fori_loop(i * chunks // 3, (i + 1) * chunks // 3, c_step, 0)

    lax.fori_loop(pause, chunks, x_step, 0)

    @pl.when(me > 0)
    def _():
        gains_0()
        lax.fori_loop(0, chunks, rest_step, 0)
        gains_1()
        gains_2()
        gains_3()

    rows_copy().wait_send()
    segs_copy().wait_send()
    gp_copy().wait_send()
    for d in range(1, ALONG_X):
        gx_copy(d).wait_send()
    for d in range(1, along_y):
        gy_copy(d).wait_send()
    for h in range(each):

        @pl.when(me >= my_y + along_y * h)
        def _():
            for d in range(1, along_y):
                by_copy(h, d).wait_send()

            @pl.when(me < last)
            def _():
                for p in range(PIECES):
                    z_copy(h, p).wait_send()

    def done_b(t, carry):
        for d in range(1, ALONG_X):
            bx_copy(t, d).wait_send()
        bc_copy(t).wait_send()
        return carry

    lax.fori_loop(0, me + 1, done_b, 0)

    @pl.when(me < last)
    def _():
        def done_a(t, carry):
            a_relay(t).wait_send()
            return carry

        lax.fori_loop(0, me + 1, done_a, 0)
        n_copy().wait_send()

        def done_x(k, carry):
            x_copy(k).wait_send()
            return carry

        lax.fori_loop(0, chunks, done_x, 0)

    @pl.when(me > 0)
    def _():
        def done_f(t, carry):
            f_copy(t).wait_send()
            return carry

        lax.fori_loop(0, me, done_f, 0)
        s_copy().wait_send()

        def done_c(k, carry):
            c_copy(k).wait_send()
            return carry

        lax.fori_loop(0, chunks, done_c, 0)


def run_chain(sections, along_y, row_len, rows, segs, wqkv, wout, gain, cot):
    tokens, width = cot.shape
    head = wout.shape[0]
    chunks = width // CHUNK
    each = sections // along_y
    blocks = head // BLOCK
    vmem = pl.BlockSpec(memory_space=pltpu.VMEM)
    dma = pltpu.SemaphoreType.DMA
    square = (head, tokens)
    return pl.pallas_call(
        functools.partial(chain_kernel, sections, along_y, row_len),
        out_shape=(
            jax.ShapeDtypeStruct((tokens, width), BF16),
            jax.ShapeDtypeStruct((chunks, CHUNK), F32),
        ),
        in_specs=[vmem] * 6,
        out_specs=(vmem, vmem),
        scratch_shapes=[
            pltpu.VMEM(rows.shape, BF16),
            pltpu.VMEM(segs.shape, BF16),
            pltpu.VMEM((each, PIECES, BLOCK, width // PIECES), BF16),
            pltpu.VMEM((sections, blocks, BLOCK, 4 * head), BF16),
            pltpu.VMEM((sections, 4 * head, head), BF16),
            pltpu.VMEM((4 * head, tokens), F32),
            pltpu.VMEM(square, F32),
            pltpu.VMEM((tokens, tokens), F32),
            pltpu.VMEM((sections, *square), BF16),
            pltpu.VMEM(square, BF16),
            pltpu.VMEM((8, tokens), F32),
            pltpu.VMEM((8, tokens), F32),
            pltpu.VMEM((sections, *square), BF16),
            pltpu.VMEM((sections, *square), BF16),
            pltpu.VMEM((8, tokens), F32),
            pltpu.VMEM((8, tokens), F32),
            pltpu.VMEM((chunks, tokens, CHUNK), BF16),
            pltpu.VMEM((chunks, tokens, CHUNK), BF16),
            pltpu.VMEM((chunks, tokens, CHUNK), BF16),
            pltpu.VMEM((chunks, tokens, CHUNK), BF16),
            pltpu.VMEM((4 * head, tokens), BF16),
            pltpu.VMEM((tokens, 4 * head), BF16),
            pltpu.VMEM((tokens, head), BF16),
            pltpu.VMEM((tokens, tokens), F32),
            pltpu.VMEM(square, F32),
            pltpu.VMEM(square, F32),
            pltpu.VMEM(square, F32),
            pltpu.VMEM((tokens, tokens), F32),
            pltpu.VMEM(square, F32),
            pltpu.VMEM((8, tokens), F32),
            pltpu.VMEM((chunks, CHUNK), F32),
            pltpu.VMEM((chunks, CHUNK), F32),
            pltpu.VMEM((ALONG_X, chunks, CHUNK), F32),
            pltpu.VMEM((along_y, chunks, CHUNK), F32),
            dma((2,)), dma((2,)), dma((each, PIECES)), dma((each, PIECES)),
            dma((each, along_y)), dma((sections,)),
            dma((sections, ALONG_X)), dma((sections, ALONG_X)),
            dma((sections,)), dma((sections,)),
            dma((sections,)), dma((sections,)), dma, dma,
            dma((sections,)), dma((sections,)), dma, dma,
            dma((chunks,)), dma((chunks,)), dma((chunks,)), dma((chunks,)),
            dma, dma, dma((ALONG_X,)), dma((ALONG_X,)), dma((along_y,)), dma((along_y,)),
        ],
        compiler_params=pltpu.CompilerParams(
            collective_id=0, has_side_effects=True, vmem_limit_bytes=48 << 20
        ),
    )(rows, segs, wqkv, wout, gain, cot)


def local(tokens_in, cotangent, gains, w_qkv, w_out, segments, plan):
    sections = lax.axis_size("section")
    along_y = lax.axis_size("dp") // ALONG_X
    core = lax.axis_index("group")
    rows_dev = plan.shape[1]
    width = tokens_in.shape[1]
    row_len = segments.shape[1]
    half = rows_dev // 2 * row_len

    order = plan[0]
    blocks = tokens_in.reshape(rows_dev, row_len, width)
    rows = blocks.at[order].get(mode="promise_in_bounds").reshape(2, half, width)
    segs = segments.at[order].get(mode="promise_in_bounds").astype(BF16).reshape(2, half)
    spot = jnp.arange(2 * half) // half == core
    segs = jnp.where(spot[None], jnp.concatenate([segs, segs], axis=1), 0)
    segs = jnp.broadcast_to(segs[:, None, :], (2, 16, 2 * half))

    grads, gain_whole = run_chain(
        sections, along_y, row_len, rows, segs, w_qkv[0], w_out[0], gains, cotangent
    )
    return grads[None], gain_whole.reshape(1, width)


def solution(mesh):
    placed = (
        P(("dp", "group"), None),
        P(("dp", "group"), None),
        P("section", None),
        P("section", None, None),
        P("section", None, None),
        P(("dp", "group"), None),
        P(("dp", "group"), None),
    )
    return jax.shard_map(
        local,
        mesh=mesh,
        in_specs=placed,
        out_specs=(P("section", ("dp", "group"), None), P("section", None)),
        check_vma=False,
    )
```

```python
import functools
import math

import jax
import jax.numpy as jnp
from jax import lax
from jax.experimental import pallas as pl
from jax.experimental.pallas import tpu as pltpu
from jax.sharding import PartitionSpec as P

MESH = pl.DeviceIdType.MESH
F32 = jnp.float32
BF16 = jnp.bfloat16
CHUNK = 128
BLOCK = 16
PIECES = 4
ALONG_X = 4
AHEAD = 8
LAG = 3


def nn(a, b):
    return lax.dot_general(a, b, (((1,), (0,)), ((), ())), preferred_element_type=F32)


def nt(a, b):
    return lax.dot_general(a, b, (((1,), (1,)), ((), ())), preferred_element_type=F32)


def chain_kernel(
    sections, along_y, row_len,
    rows_ref, segs_ref, wqkv_hbm, wout_hbm, gain_hbm, cot_hbm,
    out_hbm, gtotal_ref,
    wqkv_ref, wout_ref, gain_ref, cot_ref, out_ref, x0, seg_in, zb, bg, bgt, zt, et, bias, a_in, a_own, n_in, n_out, f_in, f_out, s_in, s_out,
    x_in, x_out, c_in, c_out,
    mt, m_tok, a_tok, sum_cols,
    q_s, k_s, v_s, p_s, y_s, r_s,
    g_own, g_pair, g_x, g_y,
    e_send, e_recv, z_send, z_recv, by_send, by_recv, bx_send, bx_recv, bc_send, bc_recv,
    a_send, a_recv, n_send, n_recv, f_send, f_recv, s_send, s_recv,
    x_send, x_recv, c_send, c_recv,
    gp_send, gp_recv, gx_send, gx_recv, gy_send, gy_recv,
    in_sem, out_sem, pair_sem,
):
    me = lax.axis_index("section")
    place = lax.axis_index("dp")
    core = lax.axis_index("group")
    my_y, my_x = lax.div(place, ALONG_X), lax.rem(place, ALONG_X)
    last = sections - 1
    up = lax.rem(me + 1, sections)
    down = lax.rem(me + sections - 1, sections)
    other = 1 - core
    head = a_own.shape[0]
    chunks, tokens, wide = x_in.shape
    width = chunks * wide
    each = sections // along_y
    mine = core * ALONG_X + my_x
    scale = 1.0 / math.sqrt(head)

    def y_peer(d):
        return lax.rem(my_y + d, along_y) * ALONG_X + my_x

    def x_peer(d):
        return my_y * ALONG_X + lax.rem(my_x + d, ALONG_X)

    loads = [
        pltpu.make_async_copy(src, dst, in_sem.at[i])
        for i, (src, dst) in enumerate(
            [
                (wout_hbm, wout_ref), (cot_hbm, cot_ref), (gain_hbm, gain_ref),
                (wqkv_hbm, wqkv_ref),
            ]
        )
    ]
    for load in loads:
        load.start()

    barrier = pltpu.get_barrier_semaphore()
    peers = [{"group": other}]
    peers += [{"dp": y_peer(d)} for d in range(1, along_y)]
    peers += [{"dp": x_peer(d)} for d in range(1, ALONG_X)]
    for peer in peers:
        pl.semaphore_signal(barrier, inc=1, device_id=peer, device_id_type=MESH)

    @pl.when(me < last)
    def _():
        pl.semaphore_signal(barrier, inc=1, device_id={"section": up}, device_id_type=MESH)

    @pl.when(me > 0)
    def _():
        pl.semaphore_signal(barrier, inc=1, device_id={"section": down}, device_id_type=MESH)

    def copy_to(src, dst, ssem, rsem, where):
        return pltpu.make_async_remote_copy(
            src_ref=src, dst_ref=dst, send_sem=ssem, recv_sem=rsem,
            device_id=where, device_id_type=MESH,
        )

    def rows_copy():
        return copy_to(
            rows_ref.at[other], x0.at[core], e_send.at[0], e_recv.at[0], {"group": other}
        )

    def segs_copy():
        return copy_to(
            segs_ref.at[other], seg_in.at[core], e_send.at[1], e_recv.at[1], {"group": other}
        )

    def z_copy(h, p):
        return copy_to(
            zb.at[h, p], zb.at[h, p], z_send.at[h, p], z_recv.at[h, p], {"section": up}
        )

    def by_copy(h, d):
        t = my_y + along_y * h
        return copy_to(
            bg.at[t, mine], bg.at[t, mine], by_send.at[h, d], by_recv.at[t], {"dp": y_peer(d)}
        )

    def by_arrival(t):
        return copy_to(
            bg.at[t, mine], bg.at[t, mine], by_send.at[0, 0], by_recv.at[t], {"dp": y_peer(1)}
        )

    def bx_copy(t, d):
        return copy_to(
            bg.at[t, mine], bg.at[t, mine], bx_send.at[t, d], bx_recv.at[t, d], {"dp": x_peer(d)}
        )

    def bc_copy(t):
        half = pl.ds(core * ALONG_X, ALONG_X)
        return copy_to(
            bg.at[t, half], bg.at[t, half], bc_send.at[t], bc_recv.at[t], {"group": other}
        )

    def a_relay(t):
        return copy_to(a_in.at[t], a_in.at[t], a_send.at[t], a_recv.at[t], {"section": up})

    def a_first():
        return copy_to(a_own, a_in.at[me], a_send.at[me], a_recv.at[me], {"section": up})

    def n_copy():
        return copy_to(n_out, n_in, n_send, n_recv, {"section": up})

    def f_copy(t):
        return copy_to(f_out.at[t], f_in.at[t], f_send.at[t], f_recv.at[t], {"section": down})

    def s_copy():
        return copy_to(s_out, s_in, s_send, s_recv, {"section": down})

    def x_copy(k):
        return copy_to(x_out.at[k], x_in.at[k], x_send.at[k], x_recv.at[k], {"section": up})

    def lanes(k):
        return pl.ds(pl.multiple_of(k * wide, wide), wide)

    def c_copy(k):
        return copy_to(
            c_out.at[k], c_in.at[k], c_send.at[k], c_recv.at[k], {"section": down}
        )

    def gp_copy():
        return copy_to(g_own, g_pair, gp_send, gp_recv, {"group": other})

    def gx_copy(d):
        return copy_to(
            g_x.at[my_x], g_x.at[my_x], gx_send.at[d], gx_recv.at[d], {"dp": x_peer(d)}
        )

    def gy_copy(d):
        return copy_to(
            g_y.at[my_y], g_y.at[my_y], gy_send.at[d], gy_recv.at[d], {"dp": y_peer(d)}
        )

    def block_of(t):
        return bg[t].reshape(head, 4 * head)

    def o_copy(k):
        part = lanes(k)
        return pltpu.make_async_copy(out_ref.at[:, part], out_hbm.at[:, part], out_sem.at[k])

    def tell_pair(i):
        pl.semaphore_signal(
            pair_sem.at[i], inc=1, device_id={"group": other}, device_id_type=MESH
        )

    piece = width // PIECES
    loads[0].wait()
    for h in range(each):

        @pl.when(me == my_y + along_y * h)
        def _():
            start = pl.multiple_of(mine * BLOCK, BLOCK)
            for p in range(PIECES):
                zb[h, p] = wout_ref[pl.ds(start, BLOCK), p * piece : (p + 1) * piece]

    along_z = jnp.where(me < last, 1, 0) + jnp.where(me > 0, 1, 0)
    pl.semaphore_wait(barrier, len(peers) + along_z)
    rows_copy().start()
    segs_copy().start()
    for h in range(each):

        @pl.when((me == my_y + along_y * h) & (me < last))
        def _():
            for p in range(PIECES):
                z_copy(h, p).start()

    x0[core] = rows_ref[core]
    seg_in[core] = segs_ref[core]
    loads[1].wait()
    et[...] = nt(wout_ref[...], cot_ref[...])

    @pl.when(me == last)
    def _():
        for k in range(chunks):
            c_in[k] = cot_ref[:, k * wide : (k + 1) * wide]
        s_in[...] = jnp.zeros_like(s_in)
        f_in[last] = jnp.zeros_like(f_in[last])

    loads[2].wait()
    loads[3].wait()
    rows_copy().wait_recv()
    segs_copy().wait_recv()

    segment = seg_in[0][0:8, :].astype(F32) + seg_in[1][0:8, :].astype(F32)
    of_query = jnp.broadcast_to(segment[0:1, :], (tokens, tokens))
    of_key = of_query.T
    key = lax.broadcasted_iota(jnp.int32, (tokens, tokens), 0)
    query = lax.broadcasted_iota(jnp.int32, (tokens, tokens), 1)
    allowed = (key <= query) & (key // row_len == query // row_len) & (of_key == of_query)
    bias[...] = jnp.where(allowed, 0.0, -1e30)

    square = jnp.zeros((tokens, 128), F32)
    grown = jnp.zeros((tokens, 3 * head), F32)
    outer = jnp.zeros((head, tokens), F32)
    for p in range(PIECES):
        cut = slice(p * piece, (p + 1) * piece)
        x = x0[:, :, cut].reshape(tokens, piece)
        wide_x = x.astype(F32)
        grown += nn((wide_x * gain_ref[0:1, cut]).astype(BF16), wqkv_ref[cut, :])
        outer += nt(wout_ref[:, cut], x)
        for i in range(piece // 128):
            part = wide_x[:, i * 128 : (i + 1) * 128]
            square += part * part
    zt[0 : 3 * head, :] = grown.T
    zt[3 * head :, :] = outer

    @pl.when(me == 0)
    def _():
        n_in[...] = jnp.sum(square.T, axis=0, keepdims=True) + jnp.zeros_like(n_in)
        for k in range(chunks):
            x_in[k] = x0[:, :, k * wide : (k + 1) * wide].reshape(tokens, wide)

    for h in reversed(range(each)):
        source = my_y + along_y * h

        @pl.when(me > source)
        def _():
            for p in range(PIECES):
                z_copy(h, p).wait_recv()

                @pl.when(me < last)
                def _():
                    z_copy(h, p).start()

        @pl.when(me >= source)
        def _():
            left = jnp.zeros((BLOCK, 3 * head), F32)
            right = jnp.zeros((BLOCK, head), F32)
            for p in range(PIECES):
                cut = slice(p * piece, (p + 1) * piece)
                rows = zb[h, p]
                left += nn((rows.astype(F32) * gain_ref[0:1, cut]).astype(BF16), wqkv_ref[cut, :])
                right += nt(rows, wout_ref[:, cut])
            bg[source, mine] = jnp.concatenate([left, right], axis=1).astype(BF16)
            for d in range(1, along_y):
                by_copy(h, d).start()

        top = jnp.minimum(me, along_y * h + along_y - 1)
        count = jnp.maximum(top - along_y * h + 1, 0)

        def flow(i, carry):
            @pl.when(i < count)
            def _():
                t = top - i

                @pl.when(lax.rem(t, along_y) != my_y)
                def _():
                    by_arrival(t).wait_recv()

                for d in range(1, ALONG_X):
                    bx_copy(t, d).start()

            @pl.when((i >= LAG) & (i < count + LAG))
            def _():
                t = top - (i - LAG)
                for d in range(1, ALONG_X):
                    bx_copy(t, d).wait_recv()
                bc_copy(t).start()

            @pl.when(i >= 2 * LAG)
            def _():
                t = top - (i - 2 * LAG)
                bc_copy(t).wait_recv()
                bgt[t] = block_of(t).T

            return carry

        lax.fori_loop(0, jnp.where(count > 0, count + 2 * LAG, 0), flow, 0)

    def gather(t, carry):
        a_relay(t).wait_recv()

        @pl.when(me < last)
        def _():
            a_relay(t).start()

        zt[...] += nn(bgt[t], a_in[t])
        return carry

    lax.fori_loop(0, me, gather, 0)

    @pl.when(me > 0)
    def _():
        n_copy().wait_recv()

    norm = n_in[0:1, :]
    scale_r = lax.rsqrt(jnp.maximum(norm, 0.0) * (1.0 / width) + 1e-05)
    qt = zt[0:head, :] * scale_r
    kt = zt[head : 2 * head, :] * scale_r
    vt = zt[2 * head : 3 * head, :] * scale_r
    yt = zt[3 * head :, :]
    scores = nn(kt.T.astype(BF16), qt.astype(BF16)) * scale + bias[...]
    top = jnp.max(scores, axis=0, keepdims=True)
    weights = jnp.exp(scores - top)
    weights = weights / jnp.sum(weights, axis=0, keepdims=True)
    mixed = nn(vt.astype(BF16), weights.astype(BF16))
    a_own[...] = mixed.astype(BF16)

    @pl.when(me < last)
    def _():
        a_first().start()

    at = a_own[...]
    self_block = block_of(me)[:, 3 * head :]
    y1 = yt + nn(self_block, at)
    moved = norm + jnp.sum(at.astype(F32) * (yt + y1), axis=0, keepdims=True)
    n_out[...] = jnp.broadcast_to(moved, n_out.shape)

    @pl.when(me < last)
    def _():
        n_copy().start()

    tell_pair(0)
    q_s[...] = qt
    k_s[...] = kt
    v_s[...] = vt
    p_s[...] = weights
    y_s[...] = y1
    r_s[...] = jnp.broadcast_to(scale_r, r_s.shape)
    a_tok[...] = at.astype(F32).T.astype(BF16)

    pl.semaphore_wait(pair_sem.at[0], 1)

    def x_step(k, carry):
        @pl.when(me > 0)
        def _():
            x_copy(k).wait_recv()

        @pl.when(me < last)
        def _():
            longer = x_in[k].astype(F32) + nn(a_tok[...], wout_ref[:, lanes(k)])
            x_out[k] = longer.astype(BF16)
            x_copy(k).start()

        return carry

    pause = jnp.minimum(chunks, AHEAD * (last - me))
    lax.fori_loop(0, pause, x_step, 0)

    @pl.when(me < last)
    def _():
        f_copy(me).wait_recv()
        s_copy().wait_recv()

    summed = s_in[0:1, :]
    dat = et[...] - summed * y_s[...] + f_in[me].astype(F32)
    datb = dat.astype(BF16)
    pt = p_s[...]
    dvt = nt(datb, pt.astype(BF16))
    dpt = nn(v_s[...].T.astype(BF16), datb)
    dst = pt * (dpt - jnp.sum(pt * dpt, axis=0, keepdims=True)) * scale
    dstb = dst.astype(BF16)
    dqt = nn(k_s[...].astype(BF16), dstb)
    dkt = nt(q_s[...].astype(BF16), dstb)
    r = r_s[0:1, :]
    inner = jnp.sum(q_s[...] * dqt + k_s[...] * dkt + v_s[...] * dvt, axis=0, keepdims=True)
    beta = r * r * (1.0 / width) * inner
    mt[0:head, :] = (r * dqt).astype(BF16)
    mt[head : 2 * head, :] = (r * dkt).astype(BF16)
    mt[2 * head : 3 * head, :] = (r * dvt).astype(BF16)
    mt[3 * head :, :] = (-summed * a_own[...].astype(F32)).astype(BF16)
    s_out[...] = jnp.broadcast_to(summed + beta, s_out.shape)

    def f_step(i, carry):
        t = me - 1 - i

        @pl.when(me < last)
        def _():
            f_copy(t).wait_recv()

        @pl.when(me == last)
        def _():
            f_in[t] = jnp.zeros_like(f_in[t])

        f_out[t] = (f_in[t].astype(F32) + nn(block_of(t), mt[...])).astype(BF16)
        f_copy(t).start()

        return carry

    lax.fori_loop(0, jnp.minimum(me, 1), f_step, 0)

    @pl.when(me > 0)
    def _():
        s_copy().start()

    tell_pair(1)
    pl.semaphore_wait(pair_sem.at[1], 1)
    lax.fori_loop(1, me, f_step, 0)

    for i in range(4):
        part = slice(i * head, (i + 1) * head)
        m_tok[:, part] = mt[part, :].astype(F32).T.astype(BF16)
    sum_cols[...] = jnp.broadcast_to(summed + beta, (tokens, tokens)).T

    def turned(k):
        start = pl.multiple_of(k * wide, wide)
        return nt(m_tok[:, 0 : 3 * head], wqkv_ref[pl.ds(start, wide), :])

    def gain_of(k, value):
        g_own[pl.ds(k, 1), :] = jnp.sum(x_in[k].astype(F32) * value, axis=0, keepdims=True)

    def gain_step(k, carry):
        gain_of(k, turned(k))
        return carry

    def finish(k, value):
        out_ref[:, lanes(k)] = (value - sum_cols[...] * x_in[k].astype(F32)).astype(BF16)
        o_copy(k).start()

    late = last - chunks // AHEAD + 1

    def gains_0():
        lax.fori_loop(0, jnp.where((me == 0) | (me >= late), chunks, 0), gain_step, 0)
        gp_copy().start()

    def gains_1():
        gp_copy().wait_recv()
        g_x[my_x] = g_own[...] + g_pair[...]
        for d in range(1, ALONG_X):
            gx_copy(d).start()

    def gains_2():
        for d in range(1, ALONG_X):
            gx_copy(d).wait_recv()
        total = g_x[0]
        for i in range(1, ALONG_X):
            total += g_x[i]
        g_y[my_y] = total
        for d in range(1, along_y):
            gy_copy(d).start()

    def gains_3():
        for d in range(1, along_y):
            gy_copy(d).wait_recv()
        total = g_y[0]
        for i in range(1, along_y):
            total += g_y[i]
        gtotal_ref[...] = total

    def c_step(k, carry):
        @pl.when(me < last)
        def _():
            c_copy(k).wait_recv()

        value = turned(k)
        fresh = c_in[k].astype(F32) + gain_ref[0:1, lanes(k)] * value
        fresh += nn(m_tok[:, 3 * head :], wout_ref[:, lanes(k)])

        @pl.when(me > 0)
        def _():
            c_out[k] = fresh.astype(BF16)
            c_copy(k).start()

        @pl.when(me < late)
        def _():
            finish(k, fresh)

        @pl.when((me > 0) & (me < late))
        def _():
            gain_of(k, value)

        return carry

    def rest_step(k, carry):
        finish(k, c_out[k].astype(F32))
        return carry

    stages = (gains_0, gains_1, gains_2, gains_3)
    for i, stage in enumerate(stages):
        pl.when(me == 0)(stage)
        if i < 3:
            lax.fori_loop(i * chunks // 3, (i + 1) * chunks // 3, c_step, 0)

    lax.fori_loop(pause, chunks, x_step, 0)

    @pl.when(me > 0)
    def _():
        gains_0()
        lax.fori_loop(0, jnp.where(me >= late, chunks, 0), rest_step, 0)
        gains_1()
        gains_2()
        gains_3()

    def done_o(k, carry):
        o_copy(k).wait()
        return carry

    lax.fori_loop(0, chunks, done_o, 0)
    rows_copy().wait_send()
    segs_copy().wait_send()
    gp_copy().wait_send()
    for d in range(1, ALONG_X):
        gx_copy(d).wait_send()
    for d in range(1, along_y):
        gy_copy(d).wait_send()
    for h in range(each):

        @pl.when(me >= my_y + along_y * h)
        def _():
            for d in range(1, along_y):
                by_copy(h, d).wait_send()

            @pl.when(me < last)
            def _():
                for p in range(PIECES):
                    z_copy(h, p).wait_send()

    def done_b(t, carry):
        for d in range(1, ALONG_X):
            bx_copy(t, d).wait_send()
        bc_copy(t).wait_send()
        return carry

    lax.fori_loop(0, me + 1, done_b, 0)

    @pl.when(me < last)
    def _():
        def done_a(t, carry):
            a_relay(t).wait_send()
            return carry

        lax.fori_loop(0, me + 1, done_a, 0)
        n_copy().wait_send()

        def done_x(k, carry):
            x_copy(k).wait_send()
            return carry

        lax.fori_loop(0, chunks, done_x, 0)

    @pl.when(me > 0)
    def _():
        def done_f(t, carry):
            f_copy(t).wait_send()
            return carry

        lax.fori_loop(0, me, done_f, 0)
        s_copy().wait_send()

        def done_c(k, carry):
            c_copy(k).wait_send()
            return carry

        lax.fori_loop(0, chunks, done_c, 0)


def run_chain(sections, along_y, row_len, rows, segs, wqkv, wout, gain, cot):
    tokens, width = cot.shape
    head = wout.shape[0]
    chunks = width // CHUNK
    each = sections // along_y
    blocks = head // BLOCK
    vmem = pl.BlockSpec(memory_space=pltpu.VMEM)
    anywhere = pl.BlockSpec(memory_space=pl.ANY)
    dma = pltpu.SemaphoreType.DMA
    square = (head, tokens)
    return pl.pallas_call(
        functools.partial(chain_kernel, sections, along_y, row_len),
        out_shape=(
            jax.ShapeDtypeStruct((tokens, width), BF16),
            jax.ShapeDtypeStruct((chunks, CHUNK), F32),
        ),
        in_specs=[vmem] * 2 + [anywhere] * 4,
        out_specs=(anywhere, vmem),
        scratch_shapes=[
            pltpu.VMEM(wqkv.shape, BF16),
            pltpu.VMEM(wout.shape, BF16),
            pltpu.VMEM(gain.shape, F32),
            pltpu.VMEM(cot.shape, BF16),
            pltpu.VMEM(cot.shape, BF16),
            pltpu.VMEM(rows.shape, BF16),
            pltpu.VMEM(segs.shape, BF16),
            pltpu.VMEM((each, PIECES, BLOCK, width // PIECES), BF16),
            pltpu.VMEM((sections, blocks, BLOCK, 4 * head), BF16),
            pltpu.VMEM((sections, 4 * head, head), BF16),
            pltpu.VMEM((4 * head, tokens), F32),
            pltpu.VMEM(square, F32),
            pltpu.VMEM((tokens, tokens), F32),
            pltpu.VMEM((sections, *square), BF16),
            pltpu.VMEM(square, BF16),
            pltpu.VMEM((8, tokens), F32),
            pltpu.VMEM((8, tokens), F32),
            pltpu.VMEM((sections, *square), BF16),
            pltpu.VMEM((sections, *square), BF16),
            pltpu.VMEM((8, tokens), F32),
            pltpu.VMEM((8, tokens), F32),
            pltpu.VMEM((chunks, tokens, CHUNK), BF16),
            pltpu.VMEM((chunks, tokens, CHUNK), BF16),
            pltpu.VMEM((chunks, tokens, CHUNK), BF16),
            pltpu.VMEM((chunks, tokens, CHUNK), BF16),
            pltpu.VMEM((4 * head, tokens), BF16),
            pltpu.VMEM((tokens, 4 * head), BF16),
            pltpu.VMEM((tokens, head), BF16),
            pltpu.VMEM((tokens, tokens), F32),
            pltpu.VMEM(square, F32),
            pltpu.VMEM(square, F32),
            pltpu.VMEM(square, F32),
            pltpu.VMEM((tokens, tokens), F32),
            pltpu.VMEM(square, F32),
            pltpu.VMEM((8, tokens), F32),
            pltpu.VMEM((chunks, CHUNK), F32),
            pltpu.VMEM((chunks, CHUNK), F32),
            pltpu.VMEM((ALONG_X, chunks, CHUNK), F32),
            pltpu.VMEM((along_y, chunks, CHUNK), F32),
            dma((2,)), dma((2,)), dma((each, PIECES)), dma((each, PIECES)),
            dma((each, along_y)), dma((sections,)),
            dma((sections, ALONG_X)), dma((sections, ALONG_X)),
            dma((sections,)), dma((sections,)),
            dma((sections,)), dma((sections,)), dma, dma,
            dma((sections,)), dma((sections,)), dma, dma,
            dma((chunks,)), dma((chunks,)), dma((chunks,)), dma((chunks,)),
            dma, dma, dma((ALONG_X,)), dma((ALONG_X,)), dma((along_y,)), dma((along_y,)),
            dma((4,)), dma((chunks,)), pltpu.SemaphoreType.REGULAR((2,)),
        ],
        compiler_params=pltpu.CompilerParams(
            collective_id=0, has_side_effects=True, vmem_limit_bytes=48 << 20
        ),
    )(rows, segs, wqkv, wout, gain, cot)


def local(tokens_in, cotangent, gains, w_qkv, w_out, segments, plan):
    sections = lax.axis_size("section")
    along_y = lax.axis_size("dp") // ALONG_X
    core = lax.axis_index("group")
    rows_dev = plan.shape[1]
    width = tokens_in.shape[1]
    row_len = segments.shape[1]
    half = rows_dev // 2 * row_len

    order = plan[0]
    blocks = tokens_in.reshape(rows_dev, row_len, width)
    rows = blocks.at[order].get(mode="promise_in_bounds").reshape(2, half, width)
    segs = segments.at[order].get(mode="promise_in_bounds").astype(BF16).reshape(2, half)
    spot = jnp.arange(2 * half) // half == core
    segs = jnp.where(spot[None], jnp.concatenate([segs, segs], axis=1), 0)
    segs = jnp.broadcast_to(segs[:, None, :], (2, 16, 2 * half))

    grads, gain_whole = run_chain(
        sections, along_y, row_len, rows, segs, w_qkv[0], w_out[0], gains, cotangent
    )
    return grads[None], gain_whole.reshape(1, width)


def solution(mesh):
    placed = (
        P(("dp", "group"), None),
        P(("dp", "group"), None),
        P("section", None),
        P("section", None, None),
        P("section", None, None),
        P(("dp", "group"), None),
        P(("dp", "group"), None),
    )
    return jax.shard_map(
        local,
        mesh=mesh,
        in_specs=placed,
        out_specs=(P("section", ("dp", "group"), None), P("section", None)),
        check_vma=False,
    )
```

```python
import functools
import math

import jax
import jax.numpy as jnp
from jax import lax
from jax.experimental import pallas as pl
from jax.experimental.pallas import tpu as pltpu
from jax.sharding import PartitionSpec as P

MESH = pl.DeviceIdType.MESH
F32 = jnp.float32
BF16 = jnp.bfloat16
CHUNK = 128
BLOCK = 16
PIECES = 4
ALONG_X = 4
AHEAD = 8
LAG = 3


def nn(a, b):
    return lax.dot_general(a, b, (((1,), (0,)), ((), ())), preferred_element_type=F32)


def nt(a, b):
    return lax.dot_general(a, b, (((1,), (1,)), ((), ())), preferred_element_type=F32)


def chain_kernel(
    sections, along_y, row_len,
    rows_ref, segs_ref, wqkv_hbm, wout_hbm, gain_hbm, cot_hbm,
    out_hbm, gtotal_ref,
    wqkv_ref, wout_ref, gain_ref, cot_ref, out_ref, x0, seg_in, zb, bg, bgt, zt, et, bias, a_in, a_own, n_in, n_out, f_in, f_out, s_in, s_out,
    x_in, x_out, c_in, c_out,
    mt, m_tok, a_tok, sum_cols,
    q_s, k_s, v_s, p_s, y_s, r_s,
    g_own, g_pair, g_x, g_y,
    e_send, e_recv, z_send, z_recv, by_send, by_recv, bx_send, bx_recv, bc_send, bc_recv,
    a_send, a_recv, n_send, n_recv, f_send, f_recv, s_send, s_recv,
    x_send, x_recv, c_send, c_recv,
    gp_send, gp_recv, gx_send, gx_recv, gy_send, gy_recv,
    in_sem, out_sem, pair_sem,
):
    me = lax.axis_index("section")
    place = lax.axis_index("dp")
    core = lax.axis_index("group")
    my_y, my_x = lax.div(place, ALONG_X), lax.rem(place, ALONG_X)
    last = sections - 1
    up = lax.rem(me + 1, sections)
    down = lax.rem(me + sections - 1, sections)
    other = 1 - core
    head = a_own.shape[0]
    chunks, tokens, wide = x_in.shape
    width = chunks * wide
    each = sections // along_y
    mine = core * ALONG_X + my_x
    scale = 1.0 / math.sqrt(head)

    def y_peer(d):
        return lax.rem(my_y + d, along_y) * ALONG_X + my_x

    def x_peer(d):
        return my_y * ALONG_X + lax.rem(my_x + d, ALONG_X)

    loads = [
        pltpu.make_async_copy(src, dst, in_sem.at[i])
        for i, (src, dst) in enumerate(
            [
                (wout_hbm, wout_ref), (cot_hbm, cot_ref), (gain_hbm, gain_ref),
                (wqkv_hbm, wqkv_ref),
            ]
        )
    ]
    for load in loads:
        load.start()

    barrier = pltpu.get_barrier_semaphore()
    peers = [{"group": other}]
    peers += [{"dp": y_peer(d)} for d in range(1, along_y)]
    peers += [{"dp": x_peer(d)} for d in range(1, ALONG_X)]
    for peer in peers:
        pl.semaphore_signal(barrier, inc=1, device_id=peer, device_id_type=MESH)

    @pl.when(me < last)
    def _():
        pl.semaphore_signal(barrier, inc=1, device_id={"section": up}, device_id_type=MESH)

    @pl.when(me > 0)
    def _():
        pl.semaphore_signal(barrier, inc=1, device_id={"section": down}, device_id_type=MESH)

    def copy_to(src, dst, ssem, rsem, where):
        return pltpu.make_async_remote_copy(
            src_ref=src, dst_ref=dst, send_sem=ssem, recv_sem=rsem,
            device_id=where, device_id_type=MESH,
        )

    def rows_copy():
        return copy_to(
            rows_ref.at[other], x0.at[core], e_send.at[0], e_recv.at[0], {"group": other}
        )

    def segs_copy():
        return copy_to(
            segs_ref.at[other], seg_in.at[core], e_send.at[1], e_recv.at[1], {"group": other}
        )

    def z_copy(h, p):
        return copy_to(
            zb.at[h, p], zb.at[h, p], z_send.at[h, p], z_recv.at[h, p], {"section": up}
        )

    def by_copy(h, d):
        t = my_y + along_y * h
        return copy_to(
            bg.at[t, mine], bg.at[t, mine], by_send.at[h, d], by_recv.at[t], {"dp": y_peer(d)}
        )

    def by_arrival(t):
        return copy_to(
            bg.at[t, mine], bg.at[t, mine], by_send.at[0, 0], by_recv.at[t], {"dp": y_peer(1)}
        )

    def bx_copy(t, d):
        return copy_to(
            bg.at[t, mine], bg.at[t, mine], bx_send.at[t, d], bx_recv.at[t, d], {"dp": x_peer(d)}
        )

    def bc_copy(t):
        half = pl.ds(core * ALONG_X, ALONG_X)
        return copy_to(
            bg.at[t, half], bg.at[t, half], bc_send.at[t], bc_recv.at[t], {"group": other}
        )

    def a_relay(t):
        return copy_to(a_in.at[t], a_in.at[t], a_send.at[t], a_recv.at[t], {"section": up})

    def a_first():
        return copy_to(a_own, a_in.at[me], a_send.at[me], a_recv.at[me], {"section": up})

    def n_copy():
        return copy_to(n_out, n_in, n_send, n_recv, {"section": up})

    def f_copy(t):
        return copy_to(f_out.at[t], f_in.at[t], f_send.at[t], f_recv.at[t], {"section": down})

    def s_copy():
        return copy_to(s_out, s_in, s_send, s_recv, {"section": down})

    def x_copy(k):
        return copy_to(x_out.at[k], x_in.at[k], x_send.at[k], x_recv.at[k], {"section": up})

    def lanes(k):
        return pl.ds(pl.multiple_of(k * wide, wide), wide)

    def c_copy(k):
        return copy_to(
            c_out.at[k], c_in.at[k], c_send.at[k], c_recv.at[k], {"section": down}
        )

    def gp_copy():
        return copy_to(g_own, g_pair, gp_send, gp_recv, {"group": other})

    def gx_copy(d):
        return copy_to(
            g_x.at[my_x], g_x.at[my_x], gx_send.at[d], gx_recv.at[d], {"dp": x_peer(d)}
        )

    def gy_copy(d):
        return copy_to(
            g_y.at[my_y], g_y.at[my_y], gy_send.at[d], gy_recv.at[d], {"dp": y_peer(d)}
        )

    def block_of(t):
        return bg[t].reshape(head, 4 * head)

    def o_copy(k):
        part = lanes(k)
        return pltpu.make_async_copy(out_ref.at[:, part], out_hbm.at[:, part], out_sem.at[k])

    def tell_pair(i):
        pl.semaphore_signal(
            pair_sem.at[i], inc=1, device_id={"group": other}, device_id_type=MESH
        )

    piece = width // PIECES
    loads[0].wait()
    for h in range(each):

        @pl.when(me == my_y + along_y * h)
        def _():
            start = pl.multiple_of(mine * BLOCK, BLOCK)
            for p in range(PIECES):
                zb[h, p] = wout_ref[pl.ds(start, BLOCK), p * piece : (p + 1) * piece]

    along_z = jnp.where(me < last, 1, 0) + jnp.where(me > 0, 1, 0)
    pl.semaphore_wait(barrier, len(peers) + along_z)
    rows_copy().start()
    segs_copy().start()
    for h in range(each):

        @pl.when((me == my_y + along_y * h) & (me < last))
        def _():
            for p in range(PIECES):
                z_copy(h, p).start()

    x0[core] = rows_ref[core]
    seg_in[core] = segs_ref[core]
    loads[1].wait()
    et[...] = nt(wout_ref[...], cot_ref[...])

    @pl.when(me == last)
    def _():
        for k in range(chunks):
            c_in[k] = cot_ref[:, k * wide : (k + 1) * wide]
        s_in[...] = jnp.zeros_like(s_in)
        f_in[last] = jnp.zeros_like(f_in[last])

    loads[2].wait()
    loads[3].wait()
    rows_copy().wait_recv()
    segs_copy().wait_recv()

    segment = seg_in[0][0:8, :].astype(F32) + seg_in[1][0:8, :].astype(F32)
    of_query = jnp.broadcast_to(segment[0:1, :], (tokens, tokens))
    of_key = of_query.T
    key = lax.broadcasted_iota(jnp.int32, (tokens, tokens), 0)
    query = lax.broadcasted_iota(jnp.int32, (tokens, tokens), 1)
    allowed = (key <= query) & (key // row_len == query // row_len) & (of_key == of_query)
    bias[...] = jnp.where(allowed, 0.0, -1e30)

    square = jnp.zeros((tokens, 128), F32)
    grown = jnp.zeros((tokens, 3 * head), F32)
    outer = jnp.zeros((head, tokens), F32)
    for p in range(PIECES):
        cut = slice(p * piece, (p + 1) * piece)
        x = x0[:, :, cut].reshape(tokens, piece)
        wide_x = x.astype(F32)
        grown += nn((wide_x * gain_ref[0:1, cut]).astype(BF16), wqkv_ref[cut, :])
        outer += nt(wout_ref[:, cut], x)
        for i in range(piece // 128):
            part = wide_x[:, i * 128 : (i + 1) * 128]
            square += part * part
    zt[0 : 3 * head, :] = grown.T
    zt[3 * head :, :] = outer

    @pl.when(me == 0)
    def _():
        n_in[...] = jnp.sum(square.T, axis=0, keepdims=True) + jnp.zeros_like(n_in)
        for k in range(chunks):
            x_in[k] = x0[:, :, k * wide : (k + 1) * wide].reshape(tokens, wide)

    for h in reversed(range(each)):
        source = my_y + along_y * h

        @pl.when(me > source)
        def _():
            for p in range(PIECES):
                z_copy(h, p).wait_recv()

                @pl.when(me < last)
                def _():
                    z_copy(h, p).start()

        @pl.when(me >= source)
        def _():
            left = jnp.zeros((BLOCK, 3 * head), F32)
            right = jnp.zeros((BLOCK, head), F32)
            for p in range(PIECES):
                cut = slice(p * piece, (p + 1) * piece)
                rows = zb[h, p]
                left += nn((rows.astype(F32) * gain_ref[0:1, cut]).astype(BF16), wqkv_ref[cut, :])
                right += nt(rows, wout_ref[:, cut])
            bg[source, mine] = jnp.concatenate([left, right], axis=1).astype(BF16)
            for d in range(1, along_y):
                by_copy(h, d).start()

        top = jnp.minimum(me, along_y * h + along_y - 1)
        count = jnp.maximum(top - along_y * h + 1, 0)

        def flow(i, carry):
            @pl.when(i < count)
            def _():
                t = top - i

                @pl.when(lax.rem(t, along_y) != my_y)
                def _():
                    by_arrival(t).wait_recv()

                for d in range(1, ALONG_X):
                    bx_copy(t, d).start()

            @pl.when((i >= LAG) & (i < count + LAG))
            def _():
                t = top - (i - LAG)
                for d in range(1, ALONG_X):
                    bx_copy(t, d).wait_recv()
                bc_copy(t).start()

            @pl.when(i >= 2 * LAG)
            def _():
                t = top - (i - 2 * LAG)
                bc_copy(t).wait_recv()
                bgt[t] = block_of(t).T

            return carry

        lax.fori_loop(0, jnp.where(count > 0, count + 2 * LAG, 0), flow, 0)

    def gather(t, carry):
        a_relay(t).wait_recv()

        @pl.when(me < last)
        def _():
            a_relay(t).start()

        zt[...] += nn(bgt[t], a_in[t])
        return carry

    lax.fori_loop(0, me, gather, 0)

    @pl.when(me > 0)
    def _():
        n_copy().wait_recv()

    norm = n_in[0:1, :]
    scale_r = lax.rsqrt(jnp.maximum(norm, 0.0) * (1.0 / width) + 1e-05)
    qt = zt[0:head, :] * scale_r
    kt = zt[head : 2 * head, :] * scale_r
    vt = zt[2 * head : 3 * head, :] * scale_r
    yt = zt[3 * head :, :]
    scores = nn(kt.T.astype(BF16), qt.astype(BF16)) * scale + bias[...]
    top = jnp.max(scores, axis=0, keepdims=True)
    weights = jnp.exp(scores - top)
    weights = weights / jnp.sum(weights, axis=0, keepdims=True)
    mixed = nn(vt.astype(BF16), weights.astype(BF16))
    a_own[...] = mixed.astype(BF16)

    @pl.when(me < last)
    def _():
        a_first().start()

    at = a_own[...]
    self_block = block_of(me)[:, 3 * head :]
    y1 = yt + nn(self_block, at)
    moved = norm + jnp.sum(at.astype(F32) * (yt + y1), axis=0, keepdims=True)
    n_out[...] = jnp.broadcast_to(moved, n_out.shape)

    @pl.when(me < last)
    def _():
        n_copy().start()

    q_s[...] = qt
    k_s[...] = kt
    v_s[...] = vt
    p_s[...] = weights
    y_s[...] = y1
    r_s[...] = jnp.broadcast_to(scale_r, r_s.shape)
    a_tok[...] = at.astype(F32).T.astype(BF16)

    def x_step(k, carry):
        @pl.when(me > 0)
        def _():
            x_copy(k).wait_recv()

        @pl.when(me < last)
        def _():
            longer = x_in[k].astype(F32) + nn(a_tok[...], wout_ref[:, lanes(k)])
            x_out[k] = longer.astype(BF16)
            x_copy(k).start()

        return carry

    pause = jnp.minimum(chunks, AHEAD * (last - me))
    lax.fori_loop(0, pause, x_step, 0)

    @pl.when(me < last)
    def _():
        f_copy(me).wait_recv()
        s_copy().wait_recv()

    summed = s_in[0:1, :]
    dat = et[...] - summed * y_s[...] + f_in[me].astype(F32)
    datb = dat.astype(BF16)
    pt = p_s[...]
    dvt = nt(datb, pt.astype(BF16))
    dpt = nn(v_s[...].T.astype(BF16), datb)
    dst = pt * (dpt - jnp.sum(pt * dpt, axis=0, keepdims=True)) * scale
    dstb = dst.astype(BF16)
    dqt = nn(k_s[...].astype(BF16), dstb)
    dkt = nt(q_s[...].astype(BF16), dstb)
    r = r_s[0:1, :]
    inner = jnp.sum(q_s[...] * dqt + k_s[...] * dkt + v_s[...] * dvt, axis=0, keepdims=True)
    beta = r * r * (1.0 / width) * inner
    mt[0:head, :] = (r * dqt).astype(BF16)
    mt[head : 2 * head, :] = (r * dkt).astype(BF16)
    mt[2 * head : 3 * head, :] = (r * dvt).astype(BF16)
    mt[3 * head :, :] = (-summed * a_own[...].astype(F32)).astype(BF16)
    s_out[...] = jnp.broadcast_to(summed + beta, s_out.shape)

    def f_step(i, carry):
        t = me - 1 - i

        @pl.when(me < last)
        def _():
            f_copy(t).wait_recv()

        @pl.when(me == last)
        def _():
            f_in[t] = jnp.zeros_like(f_in[t])

        f_out[t] = (f_in[t].astype(F32) + nn(block_of(t), mt[...])).astype(BF16)
        f_copy(t).start()

        return carry

    lax.fori_loop(0, jnp.minimum(me, 1), f_step, 0)

    @pl.when(me > 0)
    def _():
        s_copy().start()

    lax.fori_loop(1, me, f_step, 0)

    for i in range(4):
        part = slice(i * head, (i + 1) * head)
        m_tok[:, part] = mt[part, :].astype(F32).T.astype(BF16)
    sum_cols[...] = jnp.broadcast_to(summed + beta, (tokens, tokens)).T

    def turned(k):
        start = pl.multiple_of(k * wide, wide)
        return nt(m_tok[:, 0 : 3 * head], wqkv_ref[pl.ds(start, wide), :])

    def gain_of(k, value):
        g_own[pl.ds(k, 1), :] = jnp.sum(x_in[k].astype(F32) * value, axis=0, keepdims=True)

    def gain_step(k, carry):
        gain_of(k, turned(k))
        return carry

    def finish(k, value):
        out_ref[:, lanes(k)] = (value - sum_cols[...] * x_in[k].astype(F32)).astype(BF16)
        o_copy(k).start()

    late = last - chunks // AHEAD + 1

    def gains_0():
        lax.fori_loop(0, jnp.where((me == 0) | (me >= late), chunks, 0), gain_step, 0)
        gp_copy().start()

    def gains_1():
        gp_copy().wait_recv()
        g_x[my_x] = g_own[...] + g_pair[...]
        for d in range(1, ALONG_X):
            gx_copy(d).start()

    def gains_2():
        for d in range(1, ALONG_X):
            gx_copy(d).wait_recv()
        total = g_x[0]
        for i in range(1, ALONG_X):
            total += g_x[i]
        g_y[my_y] = total
        for d in range(1, along_y):
            gy_copy(d).start()

    def gains_3():
        for d in range(1, along_y):
            gy_copy(d).wait_recv()
        total = g_y[0]
        for i in range(1, along_y):
            total += g_y[i]
        gtotal_ref[...] = total

    def c_step(k, carry):
        @pl.when(me < last)
        def _():
            c_copy(k).wait_recv()

        value = turned(k)
        fresh = c_in[k].astype(F32) + gain_ref[0:1, lanes(k)] * value
        fresh += nn(m_tok[:, 3 * head :], wout_ref[:, lanes(k)])

        @pl.when(me > 0)
        def _():
            c_out[k] = fresh.astype(BF16)
            c_copy(k).start()

        @pl.when(me < late)
        def _():
            finish(k, fresh)

        @pl.when((me > 0) & (me < late))
        def _():
            gain_of(k, value)

        return carry

    def rest_step(k, carry):
        finish(k, c_out[k].astype(F32))
        return carry

    stages = (gains_0, gains_1, gains_2, gains_3)
    for i, stage in enumerate(stages):
        pl.when(me == 0)(stage)
        if i < 3:
            lax.fori_loop(i * chunks // 3, (i + 1) * chunks // 3, c_step, 0)

    lax.fori_loop(pause, chunks, x_step, 0)

    @pl.when(me > 0)
    def _():
        gains_0()
        lax.fori_loop(0, jnp.where(me >= late, chunks, 0), rest_step, 0)
        gains_1()
        gains_2()
        gains_3()

    def done_o(k, carry):
        o_copy(k).wait()
        return carry

    lax.fori_loop(0, chunks, done_o, 0)
    rows_copy().wait_send()
    segs_copy().wait_send()
    gp_copy().wait_send()
    for d in range(1, ALONG_X):
        gx_copy(d).wait_send()
    for d in range(1, along_y):
        gy_copy(d).wait_send()
    for h in range(each):

        @pl.when(me >= my_y + along_y * h)
        def _():
            for d in range(1, along_y):
                by_copy(h, d).wait_send()

            @pl.when(me < last)
            def _():
                for p in range(PIECES):
                    z_copy(h, p).wait_send()

    def done_b(t, carry):
        for d in range(1, ALONG_X):
            bx_copy(t, d).wait_send()
        bc_copy(t).wait_send()
        return carry

    lax.fori_loop(0, me + 1, done_b, 0)

    @pl.when(me < last)
    def _():
        def done_a(t, carry):
            a_relay(t).wait_send()
            return carry

        lax.fori_loop(0, me + 1, done_a, 0)
        n_copy().wait_send()

        def done_x(k, carry):
            x_copy(k).wait_send()
            return carry

        lax.fori_loop(0, chunks, done_x, 0)

    @pl.when(me > 0)
    def _():
        def done_f(t, carry):
            f_copy(t).wait_send()
            return carry

        lax.fori_loop(0, me, done_f, 0)
        s_copy().wait_send()

        def done_c(k, carry):
            c_copy(k).wait_send()
            return carry

        lax.fori_loop(0, chunks, done_c, 0)


def run_chain(sections, along_y, row_len, rows, segs, wqkv, wout, gain, cot):
    tokens, width = cot.shape
    head = wout.shape[0]
    chunks = width // CHUNK
    each = sections // along_y
    blocks = head // BLOCK
    vmem = pl.BlockSpec(memory_space=pltpu.VMEM)
    anywhere = pl.BlockSpec(memory_space=pl.ANY)
    dma = pltpu.SemaphoreType.DMA
    square = (head, tokens)
    return pl.pallas_call(
        functools.partial(chain_kernel, sections, along_y, row_len),
        out_shape=(
            jax.ShapeDtypeStruct((tokens, width), BF16),
            jax.ShapeDtypeStruct((chunks, CHUNK), F32),
        ),
        in_specs=[vmem] * 2 + [anywhere] * 4,
        out_specs=(anywhere, vmem),
        scratch_shapes=[
            pltpu.VMEM(wqkv.shape, BF16),
            pltpu.VMEM(wout.shape, BF16),
            pltpu.VMEM(gain.shape, F32),
            pltpu.VMEM(cot.shape, BF16),
            pltpu.VMEM(cot.shape, BF16),
            pltpu.VMEM(rows.shape, BF16),
            pltpu.VMEM(segs.shape, BF16),
            pltpu.VMEM((each, PIECES, BLOCK, width // PIECES), BF16),
            pltpu.VMEM((sections, blocks, BLOCK, 4 * head), BF16),
            pltpu.VMEM((sections, 4 * head, head), BF16),
            pltpu.VMEM((4 * head, tokens), F32),
            pltpu.VMEM(square, F32),
            pltpu.VMEM((tokens, tokens), F32),
            pltpu.VMEM((sections, *square), BF16),
            pltpu.VMEM(square, BF16),
            pltpu.VMEM((8, tokens), F32),
            pltpu.VMEM((8, tokens), F32),
            pltpu.VMEM((sections, *square), BF16),
            pltpu.VMEM((sections, *square), BF16),
            pltpu.VMEM((8, tokens), F32),
            pltpu.VMEM((8, tokens), F32),
            pltpu.VMEM((chunks, tokens, CHUNK), BF16),
            pltpu.VMEM((chunks, tokens, CHUNK), BF16),
            pltpu.VMEM((chunks, tokens, CHUNK), BF16),
            pltpu.VMEM((chunks, tokens, CHUNK), BF16),
            pltpu.VMEM((4 * head, tokens), BF16),
            pltpu.VMEM((tokens, 4 * head), BF16),
            pltpu.VMEM((tokens, head), BF16),
            pltpu.VMEM((tokens, tokens), F32),
            pltpu.VMEM(square, F32),
            pltpu.VMEM(square, F32),
            pltpu.VMEM(square, F32),
            pltpu.VMEM((tokens, tokens), F32),
            pltpu.VMEM(square, F32),
            pltpu.VMEM((8, tokens), F32),
            pltpu.VMEM((chunks, CHUNK), F32),
            pltpu.VMEM((chunks, CHUNK), F32),
            pltpu.VMEM((ALONG_X, chunks, CHUNK), F32),
            pltpu.VMEM((along_y, chunks, CHUNK), F32),
            dma((2,)), dma((2,)), dma((each, PIECES)), dma((each, PIECES)),
            dma((each, along_y)), dma((sections,)),
            dma((sections, ALONG_X)), dma((sections, ALONG_X)),
            dma((sections,)), dma((sections,)),
            dma((sections,)), dma((sections,)), dma, dma,
            dma((sections,)), dma((sections,)), dma, dma,
            dma((chunks,)), dma((chunks,)), dma((chunks,)), dma((chunks,)),
            dma, dma, dma((ALONG_X,)), dma((ALONG_X,)), dma((along_y,)), dma((along_y,)),
            dma((4,)), dma((chunks,)), pltpu.SemaphoreType.REGULAR((2,)),
        ],
        compiler_params=pltpu.CompilerParams(
            collective_id=0, has_side_effects=True, vmem_limit_bytes=48 << 20
        ),
    )(rows, segs, wqkv, wout, gain, cot)


def local(tokens_in, cotangent, gains, w_qkv, w_out, segments, plan):
    sections = lax.axis_size("section")
    along_y = lax.axis_size("dp") // ALONG_X
    core = lax.axis_index("group")
    rows_dev = plan.shape[1]
    width = tokens_in.shape[1]
    row_len = segments.shape[1]
    half = rows_dev // 2 * row_len

    order = plan[0]
    blocks = tokens_in.reshape(rows_dev, row_len, width)
    rows = blocks.at[order].get(mode="promise_in_bounds").reshape(2, half, width)
    segs = segments.at[order].get(mode="promise_in_bounds").astype(BF16).reshape(2, half)
    spot = jnp.arange(2 * half) // half == core
    segs = jnp.where(spot[None], jnp.concatenate([segs, segs], axis=1), 0)
    segs = jnp.broadcast_to(segs[:, None, :], (2, 16, 2 * half))

    grads, gain_whole = run_chain(
        sections, along_y, row_len, rows, segs, w_qkv[0], w_out[0], gains, cotangent
    )
    return grads[None], gain_whole.reshape(1, width)


def solution(mesh):
    placed = (
        P(("dp", "group"), None),
        P(("dp", "group"), None),
        P("section", None),
        P("section", None, None),
        P("section", None, None),
        P(("dp", "group"), None),
        P(("dp", "group"), None),
    )
    return jax.shard_map(
        local,
        mesh=mesh,
        in_specs=placed,
        out_specs=(P("section", ("dp", "group"), None), P("section", None)),
        check_vma=False,
    )
```
